128 devices in a mesh: sky: 32 (over y, z, core), band: 4 (over x).
Axes of the slice: x: 4, y: 4, z: 4, core: 2. Of those that a mesh axis runs over, the one named last changes fastest.
Arguments:
- exposures: bfloat16 [32, 4, 1024, 1024], P('sky', 'band'), may hold values from -6 to 6
- inv_variance: bfloat16 [32, 4, 1024, 1024], P('sky', 'band'), may hold values from 0.25 to 4
- mask_planes: int32 [32, 4, 2, 35], P('sky', 'band'), may hold values from 0 to 1073741823, as said below
- sky_columns: int32 [32, 4, 8], replicated, may hold values from 0 to 31, as said below
- basis_rows: float32 [9, 25], replicated, may hold values from -1 to 1
- basis_cols: float32 [9, 25], replicated, may hold values from -1 to 1
- match_coeffs: float32 [32, 4, 9], P('sky', 'band'), may hold values from -2 to 2
- detect_taps: float32 [4, 31], P('band'), may hold values from 0.05 to 0.3
Outputs:
- difference: bfloat16 [32, 4, 1024, 1024], P('sky', 'band')
- detection: float32 [1024, 4096], P('band', 'sky')
The draws below stay inside these ranges and needn't reach their ends.
Inputs may be any that keep to these rules, and one draw needn't show every extreme that they name: Each row sky_columns[e, b] holds 8 consecutive sky tile columns in order, counted modulo 32; every sky tile column is covered by some exposure of every band. Bit j of mask_planes[e, b, 0, w] marks pixel column 30 w + j of that exposure as bad and bit j of mask_planes[e, b, 1, w] pixel row 30 w + j; bits past 1024 are ignored. In every draw some word has all 30 bits set.
All inputs are finite; a program needn't handle non-finite values.
Results may differ from the reference program's by a relative error of at most 0.0095.
Values may be sent and summed in bfloat16 or wider, within the bound.
A program may use at most 128 MiB of HBM per device.

```python
import math
import jax
import jax.numpy as jnp
from jax import lax

IMG = 1024
TILE = 128
NB = 9
TAPS = 25
DTAPS = 31
ET = 8
SKYCOLS = 32
EXPOSURES = 32
BANDS = 4
NWORD = 35


def draw_mask_planes(key, part):
    flags = jax.random.randint(jax.random.fold_in(key, 11), (EXPOSURES, BANDS, 2, NWORD, 30), 0, 12)
    bit_values = (flags == 0).astype(jnp.int32)
    powers = jnp.left_shift(jnp.ones((30,), jnp.int32), jnp.arange(30, dtype=jnp.int32))
    words = jnp.sum(bit_values * powers, axis=-1).astype(jnp.int32)
    word_total = EXPOSURES * BANDS * 2 * NWORD
    full_place = jax.random.randint(jax.random.fold_in(key, 13), (), 0, word_total)
    places = jnp.arange(word_total, dtype=jnp.int32).reshape(EXPOSURES, BANDS, 2, NWORD)
    all_bits = jnp.full((EXPOSURES, BANDS, 2, NWORD), 1073741823, jnp.int32)
    return jnp.where(places == full_place, all_bits, words).astype(jnp.int32)


def draw_sky_columns(key, part):
    key_start, key_deep, key_pick, key_spread, key_any = jax.random.split(jax.random.fold_in(key, 7), 5)
    column_total = SKYCOLS
    exposure_ids = jnp.arange(EXPOSURES, dtype=jnp.int32)[:, None]
    start_column = jax.random.randint(key_start, (1, BANDS), 0, column_total)
    deep_column = jax.random.randint(key_deep, (1, BANDS), 0, column_total)
    covering = (start_column + exposure_ids * ET) % column_total
    clustered = (deep_column + jax.random.randint(key_spread, (EXPOSURES, BANDS), 0, ET // 2 + 1)) % column_total
    anywhere = jax.random.randint(key_any, (EXPOSURES, BANDS), 0, column_total)
    choose_deep = jax.random.randint(key_pick, (EXPOSURES, BANDS), 0, 2) == 0
    offsets = jnp.where(choose_deep, clustered, anywhere)
    cover_count = (column_total + ET - 1) // ET
    offsets = jnp.where(exposure_ids < cover_count, covering, offsets)
    return ((offsets[:, :, None] + jnp.arange(ET, dtype=jnp.int32)[None, None, :]) % column_total).astype(jnp.int32)


def block_levels(key, extent, shards, smallest, largest):
    level = 1.0
    for dim, parts in shards:
        steps = jax.random.uniform(jax.random.fold_in(jax.random.fold_in(key, 6), dim), (parts,), jnp.float32, smallest / len(shards), largest / len(shards))
        level = level * jnp.repeat(jnp.exp(steps), extent[dim] // parts).reshape((-1,) + (1,) * (len(extent) - 1 - dim))
    return level


def normal_values(stream_key, shape, spread, reach, shards=(), kind=jnp.bfloat16):
    values = spread * jax.random.normal(stream_key, shape, jnp.float32)
    if shards:
        values = values * block_levels(stream_key, shape, shards, -0.22, 0.18)
    return jnp.clip(values, -reach, reach).astype(kind)


def setup_inputs(seed: int = 0) -> dict:
    streams_of = jax.random.split(jax.random.key(seed), 9)
    return {
        "exposures": normal_values(streams_of[0], (EXPOSURES, BANDS, IMG, IMG), 1.0, 6.0, ((0, 32), (1, 4))),
        "inv_variance": jnp.clip(jnp.exp(math.log(4.0) - 2.7725887 * jax.random.uniform(streams_of[1], (EXPOSURES, BANDS, IMG, IMG), jnp.float32) ** block_levels(streams_of[1], (EXPOSURES, BANDS, IMG, IMG), ((0, 32), (1, 4)), -0.2, 0.2)), 0.25, 4.0).astype(jnp.bfloat16),
        "mask_planes": draw_mask_planes(jax.random.fold_in(streams_of[8], 71), 0),
        "sky_columns": draw_sky_columns(jax.random.fold_in(streams_of[8], 71), 0),
        "basis_rows": normal_values(streams_of[4], (NB, TAPS), 0.2, 1.0, (), jnp.float32),
        "basis_cols": normal_values(streams_of[5], (NB, TAPS), 0.2, 1.0, (), jnp.float32),
        "match_coeffs": normal_values(streams_of[6], (EXPOSURES, BANDS, NB), 0.35, 2.0, ((0, 32), (1, 4)), jnp.float32),
        "detect_taps": jnp.clip(0.05 + 0.25 * jax.random.uniform(streams_of[7], (BANDS, DTAPS), jnp.float32) ** block_levels(streams_of[7], (BANDS, DTAPS), ((0, 4),), -0.2, 0.2), 0.05, 0.3),
    }


def rounded(values):
    return lax.optimization_barrier(values.astype(jnp.bfloat16))


def band_matrix(tap_rows, window_width):
    offsets = jnp.arange(window_width, dtype=jnp.int32)[:, None] - jnp.arange(TILE, dtype=jnp.int32)[None, :]
    selector = (offsets[:, :, None] == jnp.arange(tap_rows.shape[1], dtype=jnp.int32)[None, None, :]).astype(jnp.float32)
    return jnp.einsum("wtl,kl->kwt", selector, tap_rows.astype(jnp.float32), precision=lax.Precision.HIGHEST).astype(jnp.bfloat16)


def keep_pixels(planes, side_length):
    places = jnp.arange(side_length, dtype=jnp.int32)
    column_bits = jnp.bitwise_and(jnp.right_shift(planes[0][places // 30], places % 30), 1)
    row_bits = jnp.bitwise_and(jnp.right_shift(planes[1][places // 30], places % 30), 1)
    return jnp.logical_and(row_bits[:, None] == 0, column_bits[None, :] == 0)


def psf_match(picture, column_taps, row_taps):
    side_length = picture.shape[1]
    block_count = side_length // TILE
    margin = TAPS // 2
    width_full = TILE + 2 * margin
    padded = jnp.pad(picture, ((0, 0), (margin, margin)))
    blocks = jnp.stack([padded[:, TILE * block_index: TILE * block_index + width_full] for block_index in range(block_count)], 0)
    column_band = band_matrix(column_taps, width_full)
    column_pass = rounded(jnp.einsum("jyw,kwt->kyjt", blocks.astype(jnp.float32), column_band.astype(jnp.float32)).reshape(NB, side_length, side_length))
    row_padded = jnp.pad(column_pass, ((0, 0), (margin, margin), (0, 0)))
    row_blocks = jnp.stack([row_padded[:, TILE * block_index: TILE * block_index + width_full, :] for block_index in range(block_count)], 0)
    row_band = band_matrix(row_taps, width_full)
    summed = jnp.einsum("ikwx,kwt->itx", row_blocks.astype(jnp.float32), row_band.astype(jnp.float32))
    return summed.reshape(side_length, side_length).astype(jnp.bfloat16)


def reference(exposures, inv_variance, mask_planes, sky_columns, basis_rows, basis_cols, match_coeffs, detect_taps):
    row_taps = basis_rows.astype(jnp.bfloat16)
    count_all = EXPOSURES * BANDS

    def match_one(inputs):
        picture, variance_inv, planes, coeffs = inputs
        column_taps = (coeffs[:, None] * basis_cols).astype(jnp.bfloat16)
        matched_one = psf_match(picture, column_taps, row_taps)
        keep = keep_pixels(planes, picture.shape[0])
        weight_one = jnp.where(keep, variance_inv, jnp.zeros_like(variance_inv))
        return matched_one, weight_one

    matched, weight = lax.map(match_one, (exposures.reshape(count_all, IMG, IMG), inv_variance.reshape(count_all, IMG, IMG), mask_planes.reshape(count_all, 2, NWORD), match_coeffs.reshape(count_all, NB)))
    matched = matched.reshape(EXPOSURES, BANDS, IMG, ET, TILE).astype(jnp.float32)
    weight = weight.reshape(EXPOSURES, BANDS, IMG, ET, TILE).astype(jnp.float32)
    placer = (sky_columns[:, :, :, None] == jnp.arange(SKYCOLS, dtype=jnp.int32)[None, None, None, :]).astype(jnp.float32)
    numer = jnp.einsum("ebyct,ebcs->byst", weight * matched, placer, precision=lax.Precision.HIGHEST)
    denom = jnp.einsum("ebyct,ebcs->byst", weight, placer, precision=lax.Precision.HIGHEST)
    template = rounded(numer / jnp.maximum(denom, 1.0)).astype(jnp.float32)
    picked = jnp.einsum("byst,ebcs->ebyct", template, placer, precision=lax.Precision.HIGHEST)
    difference = (matched - picked).astype(jnp.bfloat16).reshape(EXPOSURES, BANDS, IMG, IMG)
    sky_image = template.reshape(BANDS, IMG, SKYCOLS * TILE)
    taps = detect_taps.astype(jnp.bfloat16).astype(jnp.float32)
    margin = DTAPS // 2
    smoothed = jnp.zeros_like(sky_image)
    for offset in range(DTAPS):
        smoothed = smoothed + taps[:, offset][:, None, None] * jnp.roll(sky_image, margin - offset, axis=2)
    smoothed = rounded(smoothed).astype(jnp.float32)
    padded = jnp.pad(smoothed, ((0, 0), (margin, margin), (0, 0)))
    filtered = jnp.zeros_like(smoothed)
    for offset in range(DTAPS):
        filtered = filtered + taps[:, offset][:, None, None] * padded[:, offset: offset + IMG, :]
    detection = jnp.sum(filtered * filtered, axis=0)
    return difference, detection
```

```python
import jax
import jax.numpy as jnp
from jax import lax
from jax.experimental import pallas as pl
from jax.experimental.pallas import tpu as pltpu
from jax.sharding import PartitionSpec as P

TILE = 128
NB = 9
TAPS = 25
DTAPS = 31
IMG = 1024
HALO = 12
STRIP = NB * 16
KROWS = 10 * STRIP
NCHUNK = 8
MESH = pl.DeviceIdType.MESH
F32 = jnp.float32
BF16 = jnp.bfloat16


def rows_of(block):
    return pl.ds(pl.multiple_of(block * TILE, TILE), TILE)


def lanes_of(block):
    return pl.ds(pl.multiple_of(block * TILE, TILE), TILE)


def device_of(half, klass, slot):
    first = 8 * slot + klass
    second = 8 * lax.div(klass, 2) + 2 * slot + lax.rem(klass, 2)
    return jnp.where(half == 0, first, second)


def place(half):
    own = lax.axis_index("sky")
    y, rest = lax.div(own, 8), lax.rem(own, 8)
    z, core = lax.div(rest, 2), lax.rem(rest, 2)
    klass = jnp.where(half == 0, rest, 2 * y + core)
    slot = jnp.where(half == 0, y, z)
    return klass, slot


def row_block(step):
    half = lax.rem(step, 2)
    return half, lax.div(step, 2) + 4 * half


def turned(tiles, amount):
    for bit in (1, 2, 4):
        take = jnp.bitwise_and(jnp.full(tiles[0].shape, amount, jnp.int32), bit) != 0
        tiles = [jnp.where(take, tiles[(i + bit) % 8], tiles[i]) for i in range(8)]
    return tiles


def bit_lanes(planes_ref, plane):
    lane = lax.broadcasted_iota(jnp.int32, (8, IMG), 1)
    word = jnp.zeros((8, IMG), jnp.int32)
    first = jnp.zeros((8, IMG), jnp.int32)
    for index in range(35):
        inside = lane >= 30 * index
        word = jnp.where(inside, planes_ref[plane, index], word)
        first = jnp.where(inside, 30 * index, first)
    bit = jnp.bitwise_and(lax.shift_right_logical(word, lane - first), 1)
    return (1 - bit).astype(F32)


def build_taps(cols_ref, rows_ref, coeff_ref, col_mat, row_mat):
    pad = jnp.zeros((1, TILE - TAPS), F32)
    far = jnp.zeros((1, TILE), F32)
    for k in range(NB):
        taps = (cols_ref[k : k + 1, :] * coeff_ref[0, k]).astype(BF16).astype(F32)
        base = pltpu.roll(jnp.concatenate([taps, pad, far], 1), 2 * TILE - HALO, 1)
        ring = pltpu.roll(jnp.broadcast_to(base, (TILE, 2 * TILE)), 0, 1, stride=1, stride_axis=0)
        col_mat[:, k * TILE : (k + 1) * TILE] = ring.T.astype(BF16)
    place_w = lax.broadcasted_iota(jnp.int32, (TILE, 512), 0)
    place_l = lax.broadcasted_iota(jnp.int32, (TILE, 512), 1)
    picker = jnp.where(
        jnp.logical_and(place_l == lax.div(place_w, 16) * STRIP + lax.rem(place_w, 16), place_w < 48),
        1.0,
        0.0,
    ).astype(BF16)
    stacked = []
    for k in range(NB):
        taps = rows_ref[k : k + 1, :].astype(BF16).astype(F32)
        base = pltpu.roll(jnp.concatenate([taps, pad], 1), 4, 1)
        stacked.append(pltpu.roll(jnp.broadcast_to(base, (16, TILE)), 0, 1, stride=1, stride_axis=0))
    spread = jnp.dot(
        jnp.concatenate(stacked, 0).astype(BF16), picker, preferred_element_type=F32
    )
    first = jnp.zeros((16, 512), F32)
    for k in range(NB):
        first = first + pltpu.roll(spread[16 * k : 16 * k + 16], 16 * k, 1)
    first = jnp.concatenate([first, jnp.zeros((16, 1024), F32)], 1)
    for u in range(8):
        row_mat[16 * u : 16 * u + 16, :] = pltpu.roll(first, STRIP * u, 1)[:, :KROWS].astype(BF16)


def column_pass(picture, col_mat, mid):
    mid[0] = jnp.zeros((NB, 16, IMG), BF16)
    mid[65] = jnp.zeros((NB, 16, IMG), BF16)
    near = lax.broadcasted_iota(jnp.int32, (IMG, TILE), 1) < 64

    def one(j, _):
        here = picture[:, lanes_of(j)]
        after = picture[:, lanes_of(jnp.minimum(j + 1, 7))]
        before = picture[:, lanes_of(jnp.maximum(j - 1, 0))]
        zero = jnp.zeros_like(here)
        after = jnp.where(jnp.broadcast_to(j < 7, near.shape), after, zero)
        before = jnp.where(jnp.broadcast_to(j > 0, near.shape), before, zero)
        lhs = jnp.concatenate([here, jnp.where(near, after, before)], 1)
        for k in range(0, NB, 2):
            count = min(2, NB - k)
            got = jnp.dot(
                lhs, col_mat[:, k * TILE : (k + count) * TILE], preferred_element_type=F32
            ).astype(BF16)
            for t in range(count):
                mid[1:65, k + t, :, lanes_of(j)] = got[:, t * TILE : (t + 1) * TILE].reshape(64, 16, TILE)
        return 0

    lax.fori_loop(0, 8, one, 0)


def coadd_kernel(
    picture_in,
    variance_in,
    planes_ref,
    sky_ref,
    rows_ref,
    cols_ref,
    coeff_ref,
    difference_out,
    template_out,
    picture,
    variance,
    col_keep,
    row_keep,
    col_mat,
    row_mat,
    mid,
    matched,
    w_send,
    w_recv,
    m_send,
    m_recv,
    p_send,
    p_recv,
    numer_own,
    denom_own,
    t_all,
    q_send,
    q_recv,
    flat_ref,
    d_out,
    load_sem,
    out_sem,
    send_sem,
    w_sem,
    m_sem,
    p_sem,
    t_sem,
    q_sem,
):
    own = lax.axis_index("sky")
    band = lax.axis_index("band")
    barrier = pltpu.get_barrier_semaphore()
    for half in range(2):
        klass, slot = place(half)
        for d in range(1, 8):
            peer = device_of(half, lax.rem(klass + d, 8), slot)
            pl.semaphore_signal(barrier, inc=1, device_id=(peer, band), device_id_type=MESH)
    load_variance = pltpu.make_async_copy(variance_in, variance, load_sem.at[0])
    load_picture = pltpu.make_async_copy(picture_in, picture, load_sem.at[1])
    load_variance.start()
    load_picture.start()
    start = sky_ref[own, band, 0]
    col_keep[...] = bit_lanes(planes_ref, 0)
    row_keep[...] = bit_lanes(planes_ref, 1)
    load_variance.wait()
    pl.semaphore_wait(barrier, 14)

    def send(src, dst, sem_send, sem_recv, device):
        pltpu.make_async_remote_copy(
            src_ref=src,
            dst_ref=dst,
            send_sem=sem_send,
            recv_sem=sem_recv,
            device_id=(device, band),
            device_id_type=MESH,
        ).start()

    def wait_for(ref, sem):
        pltpu.make_async_copy(ref, ref, sem).wait()

    def to_group(step, src, dst, sem_send, sem_recv):
        half, block = row_block(step)
        klass, slot = place(half)
        for d in range(1, 8):
            peer = device_of(half, lax.rem(klass + d, 8), slot)
            send(src.at[d, rows_of(block)], dst.at[d, rows_of(block)], sem_send, sem_recv.at[step], peer)

    def stage_weight(step, _):
        half, block = row_block(step)
        klass, slot = place(half)
        flat_ref[...] = jnp.broadcast_to(row_keep[0:1, lanes_of(block)], (TILE, TILE)).T

        def part(r, _):
            at = pl.ds(pl.multiple_of(block * TILE + r * 32, 32), 32)
            flat = flat_ref[pl.ds(pl.multiple_of(r * 32, 32), 32), :]
            tiles = []
            for c in range(8):
                keep = flat * col_keep[0:1, c * TILE : (c + 1) * TILE]
                tiles.append(
                    (variance[at, c * TILE : (c + 1) * TILE].astype(F32) * keep).astype(BF16)
                )
            for d, tile in enumerate(turned(tiles, klass - start + 32)):
                w_send[d, at, :] = tile
            return 0

        lax.fori_loop(0, 4, part, 0)
        to_group(step, w_send, w_recv, send_sem.at[0], w_sem)
        return 0

    lax.fori_loop(0, NCHUNK, stage_weight, 0)
    build_taps(cols_ref, rows_ref, coeff_ref, col_mat, row_mat)
    load_picture.wait()
    column_pass(picture, col_mat, mid)

    def stage_matched(step, _):
        half, block = row_block(step)
        klass, slot = place(half)
        window = mid[pl.ds(block * 8, 10)].reshape(KROWS, IMG)
        matched[...] = jnp.dot(row_mat[...], window, preferred_element_type=F32).astype(BF16)

        def part(r, _):
            at = pl.ds(pl.multiple_of(block * TILE + r * 32, 32), 32)
            inner = pl.ds(pl.multiple_of(r * 32, 32), 32)
            tiles = [matched[inner, c * TILE : (c + 1) * TILE] for c in range(8)]
            for d, tile in enumerate(turned(tiles, klass - start + 32)):
                m_send[d, at, :] = tile
            return 0

        lax.fori_loop(0, 4, part, 0)
        to_group(step, m_send, m_recv, send_sem.at[1], m_sem)
        return 0

    lax.fori_loop(0, NCHUNK, stage_matched, 0)

    def column_slot(exposure, klass):
        begin = sky_ref[exposure, band, 0]
        c = jnp.bitwise_and(klass - begin + 32, 7)
        return lax.shift_right_logical(jnp.bitwise_and(begin + c, 31), 3)

    def reduce_group(step, _):
        half, block = row_block(step)
        klass, slot = place(half)
        wait_for(w_recv.at[pl.ds(1, 7), rows_of(block)], w_sem.at[step])
        wait_for(m_recv.at[pl.ds(1, 7), rows_of(block)], m_sem.at[step])
        rel = []
        for d in range(8):
            source = device_of(half, lax.rem(klass - d + 8, 8), slot)
            rel.append(jnp.full((32, TILE), jnp.bitwise_and(column_slot(source, klass) - slot + 4, 3), jnp.int32))

        def part(r, _):
            at = pl.ds(pl.multiple_of(block * TILE + r * 32, 32), 32)
            inner = pl.ds(pl.multiple_of(r * 32, 32), 32)
            numer = [jnp.zeros((32, TILE), F32) for _ in range(4)]
            denom = [jnp.zeros((32, TILE), F32) for _ in range(4)]
            for d in range(8):
                w = (w_recv if d else w_send)[d, at, :].astype(F32)
                wm = w * (m_recv if d else m_send)[d, at, :].astype(F32)
                for t in range(4):
                    hit = rel[d] == t
                    numer[t] = numer[t] + jnp.where(hit, wm, 0.0)
                    denom[t] = denom[t] + jnp.where(hit, w, 0.0)
            numer_own[at, :] = numer[0]
            denom_own[at, :] = denom[0]
            for t in range(1, 4):
                p_send[t, block, 0, inner, :] = numer[t].astype(BF16)
                p_send[t, block, 1, inner, :] = denom[t].astype(BF16)
            return 0

        lax.fori_loop(0, 4, part, 0)
        for t in range(1, 4):
            peer = device_of(half, klass, lax.rem(slot + t, 4))
            send(p_send.at[t, block], p_recv.at[t, block], send_sem.at[2], p_sem.at[step], peer)
        return 0

    lax.fori_loop(0, NCHUNK, reduce_group, 0)

    def make_template(step, _):
        half, block = row_block(step)
        klass, slot = place(half)
        wait_for(p_recv.at[pl.ds(1, 3), block], p_sem.at[step])
        numer = numer_own[rows_of(block), :]
        denom = denom_own[rows_of(block), :]
        for t in range(1, 4):
            numer = numer + p_recv[t, block, 0].astype(F32)
            denom = denom + p_recv[t, block, 1].astype(F32)
        t_all[0, rows_of(block), :] = (numer / jnp.maximum(denom, 1.0)).astype(BF16)
        for t in range(1, 4):
            peer = device_of(half, klass, lax.rem(slot + t, 4))
            send(t_all.at[0, rows_of(block)], t_all.at[t, rows_of(block)], send_sem.at[3], t_sem.at[step], peer)
        return 0

    lax.fori_loop(0, NCHUNK, make_template, 0)

    def pick_templates(step, _):
        half, block = row_block(step)
        klass, slot = place(half)
        wait_for(t_all.at[pl.ds(1, 3), rows_of(block)], t_sem.at[step])
        for d in range(8):
            target = device_of(half, lax.rem(klass + d, 8), slot)
            rel = jnp.full((TILE, TILE), jnp.bitwise_and(slot - column_slot(target, klass) + 4, 3), jnp.int32)
            value = t_all[0, rows_of(block), :]
            for t in range(1, 4):
                value = jnp.where(rel == t, t_all[t, rows_of(block), :], value)
            q_send[d, rows_of(block), :] = value
        to_group(step, q_send, q_recv, send_sem.at[4], q_sem)
        return 0

    lax.fori_loop(0, NCHUNK, pick_templates, 0)
    save_template = pltpu.make_async_copy(t_all.at[0], template_out, load_sem.at[2])
    save_template.start()

    def subtract(step, _):
        half, block = row_block(step)
        klass, slot = place(half)
        wait_for(q_recv.at[pl.ds(1, 7), rows_of(block)], q_sem.at[step])

        def part(r, _):
            at = pl.ds(pl.multiple_of(block * TILE + r * 32, 32), 32)
            tiles = []
            for i in range(8):
                d = (8 - i) % 8
                m = m_send[i, at, :].astype(F32)
                q = (q_recv if d else q_send)[d, at, :].astype(F32)
                tiles.append((m - q).astype(BF16))
            for c, tile in enumerate(turned(tiles, start - klass + 32)):
                d_out[at, c * TILE : (c + 1) * TILE] = tile
            return 0

        lax.fori_loop(0, 4, part, 0)
        pltpu.make_async_copy(d_out.at[rows_of(block)], difference_out.at[rows_of(block)], out_sem).start()
        return 0

    lax.fori_loop(0, NCHUNK, subtract, 0)
    save_template.wait()
    wait_for(d_out, out_sem)
    wait_for(w_send.at[pl.ds(1, 7)], send_sem.at[0])
    wait_for(m_send.at[pl.ds(1, 7)], send_sem.at[1])
    wait_for(p_send.at[pl.ds(1, 3)], send_sem.at[2])
    wait_for(t_all.at[pl.ds(1, 3)], send_sem.at[3])
    wait_for(q_send.at[pl.ds(1, 7)], send_sem.at[4])


def coadd(picture, variance, planes, sky_columns, basis_rows, basis_cols, coeffs):
    vmem = pl.BlockSpec(memory_space=pltpu.VMEM)
    smem = pl.BlockSpec(memory_space=pltpu.SMEM)
    anyw = pl.BlockSpec(memory_space=pl.ANY)
    tiles = pltpu.VMEM((8, IMG, TILE), BF16)
    parts = pltpu.VMEM((4, NCHUNK, 2, TILE, TILE), BF16)
    return pl.pallas_call(
        coadd_kernel,
        out_shape=(
            jax.ShapeDtypeStruct((IMG, IMG), BF16),
            jax.ShapeDtypeStruct((IMG, TILE), BF16),
        ),
        in_specs=[anyw, anyw, smem, smem, vmem, vmem, smem],
        out_specs=(anyw, anyw),
        scratch_shapes=[
            pltpu.VMEM((IMG, IMG), BF16),
            pltpu.VMEM((IMG, IMG), BF16),
            pltpu.VMEM((8, IMG), F32),
            pltpu.VMEM((8, IMG), F32),
            pltpu.VMEM((2 * TILE, NB * TILE), BF16),
            pltpu.VMEM((TILE, KROWS), BF16),
            pltpu.VMEM((66, NB, 16, IMG), BF16),
            pltpu.VMEM((TILE, IMG), BF16),
            tiles,
            tiles,
            tiles,
            tiles,
            parts,
            parts,
            pltpu.VMEM((IMG, TILE), F32),
            pltpu.VMEM((IMG, TILE), F32),
            pltpu.VMEM((4, IMG, TILE), BF16),
            tiles,
            tiles,
            pltpu.VMEM((TILE, TILE), F32),
            pltpu.VMEM((IMG, IMG), BF16),
            pltpu.SemaphoreType.DMA((3,)),
            pltpu.SemaphoreType.DMA,
            pltpu.SemaphoreType.DMA((5,)),
            pltpu.SemaphoreType.DMA((NCHUNK,)),
            pltpu.SemaphoreType.DMA((NCHUNK,)),
            pltpu.SemaphoreType.DMA((NCHUNK,)),
            pltpu.SemaphoreType.DMA((NCHUNK,)),
            pltpu.SemaphoreType.DMA((NCHUNK,)),
        ],
        compiler_params=pltpu.CompilerParams(
            collective_id=0, has_side_effects=True, vmem_limit_bytes=60 << 20
        ),
        name="coadd",
    )(picture, variance, planes, sky_columns, basis_rows, basis_cols, coeffs)


def with_halo(block, sides, width):
    for axis, dim in sides:
        count = lax.axis_size(axis)
        forward = [(i, (i + 1) % count) for i in range(count)]
        backward = [(target, source) for source, target in forward]
        low = lax.ppermute(
            lax.slice_in_dim(block, block.shape[dim] - width, None, axis=dim), axis, forward
        )
        high = lax.ppermute(lax.slice_in_dim(block, 0, width, axis=dim), axis, backward)
        block = jnp.concatenate([low, block, high], axis=dim)
    return block


def band_matrix(tap_rows, window_width):
    offsets = (
        jnp.arange(window_width, dtype=jnp.int32)[:, None]
        - jnp.arange(TILE, dtype=jnp.int32)[None, :]
    )
    selector = (
        offsets[:, :, None] == jnp.arange(tap_rows.shape[1], dtype=jnp.int32)[None, None, :]
    ).astype(F32)
    return jnp.einsum(
        "wtl,kl->kwt", selector, tap_rows.astype(F32), precision=lax.Precision.HIGHEST
    ).astype(BF16)


def detect(template, detect_taps):
    swap = [(8 * y + 2 * z + c, 8 * z + 2 * y + c) for y in range(4) for z in range(4) for c in range(2)]
    lower = lax.ppermute(template[512:], "sky", swap)
    template = jnp.concatenate([template[:512], lower], 0)
    margin = DTAPS // 2
    width_full = TILE + 2 * margin
    filter_band = band_matrix(detect_taps.astype(BF16), width_full)[0]
    widened = with_halo(template, (("sky", 1),), margin)
    smoothed = jnp.dot(widened, filter_band, preferred_element_type=F32).astype(BF16)
    smooth_padded = jnp.pad(smoothed, ((margin, margin), (0, 0)))
    smooth_blocks = jnp.stack(
        [smooth_padded[TILE * i : TILE * i + width_full] for i in range(8)], 0
    )
    filtered = jnp.einsum(
        "iwx,wt->itx", smooth_blocks, filter_band, preferred_element_type=F32
    ).reshape(IMG, TILE)
    power = filtered * filtered
    pieces = power.reshape(4, IMG // 4, TILE)
    arrived = lax.all_to_all(pieces, "band", split_axis=0, concat_axis=0, tiled=True)
    return arrived.sum(axis=0)


def body(
    exposures,
    inv_variance,
    mask_planes,
    sky_columns,
    basis_rows,
    basis_cols,
    match_coeffs,
    detect_taps,
):
    difference, template = coadd(
        exposures[0, 0],
        inv_variance[0, 0],
        mask_planes[0, 0],
        sky_columns,
        basis_rows,
        basis_cols,
        match_coeffs[0],
    )
    return (difference[None, None], detect(template, detect_taps))


def solution(mesh):
    in_specs = (
        P("sky", "band", None, None),
        P("sky", "band", None, None),
        P("sky", "band", None, None),
        P(),
        P(),
        P(),
        P("sky", "band", None),
        P("band", None),
    )
    out_specs = (P("sky", "band", None, None), P("band", "sky"))
    return jax.shard_map(body, mesh=mesh, in_specs=in_specs, out_specs=out_specs, check_vma=False)
```

```python
import jax
import jax.numpy as jnp
from jax import lax
from jax.experimental import pallas as pl
from jax.experimental.pallas import tpu as pltpu
from jax.sharding import PartitionSpec as P

TILE = 128
NB = 9
TAPS = 25
DTAPS = 31
IMG = 1024
HALO = 12
STRIP = NB * 16
KROWS = 10 * STRIP
NCHUNK = 8
MESH = pl.DeviceIdType.MESH
F32 = jnp.float32
BF16 = jnp.bfloat16


def rows_of(block):
    return pl.ds(pl.multiple_of(block * TILE, TILE), TILE)


def quarter_of(block):
    return pl.ds(pl.multiple_of(block * 256, 256), 256)


def lanes_of(block):
    return pl.ds(pl.multiple_of(block * TILE, TILE), TILE)


def device_of(half, klass, slot):
    first = 8 * slot + klass
    second = 8 * lax.div(klass, 2) + 2 * slot + lax.rem(klass, 2)
    return jnp.where(half == 0, first, second)


def place(half):
    own = lax.axis_index("sky")
    y, rest = lax.div(own, 8), lax.rem(own, 8)
    z, core = lax.div(rest, 2), lax.rem(rest, 2)
    klass = jnp.where(half == 0, rest, 2 * y + core)
    slot = jnp.where(half == 0, y, z)
    return klass, slot


def turned_column(column):
    y, rest = lax.div(column, 8), lax.rem(column, 8)
    return 8 * lax.div(rest, 2) + 2 * y + lax.rem(rest, 2)


def row_block(step):
    half = lax.rem(step, 2)
    return half, lax.div(step, 2) + 4 * half


def turned(tiles, amount):
    for bit in (1, 2, 4):
        take = jnp.bitwise_and(jnp.full(tiles[0].shape, amount, jnp.int32), bit) != 0
        tiles = [jnp.where(take, tiles[(i + bit) % 8], tiles[i]) for i in range(8)]
    return tiles


def bit_lanes(planes_ref, plane):
    lane = lax.broadcasted_iota(jnp.int32, (8, IMG), 1)
    word = jnp.zeros((8, IMG), jnp.int32)
    first = jnp.zeros((8, IMG), jnp.int32)
    for index in range(35):
        inside = lane >= 30 * index
        word = jnp.where(inside, planes_ref[plane, index], word)
        first = jnp.where(inside, 30 * index, first)
    bit = jnp.bitwise_and(lax.shift_right_logical(word, lane - first), 1)
    return (1 - bit).astype(F32)


def build_taps(cols_ref, rows_ref, coeff_ref, col_mat, row_mat):
    pad = jnp.zeros((1, TILE - TAPS), F32)
    far = jnp.zeros((1, TILE), F32)
    for k in range(NB):
        taps = (cols_ref[k : k + 1, :] * coeff_ref[0, k]).astype(BF16).astype(F32)
        base = pltpu.roll(jnp.concatenate([taps, pad, far], 1), 2 * TILE - HALO, 1)
        ring = pltpu.roll(jnp.broadcast_to(base, (TILE, 2 * TILE)), 0, 1, stride=1, stride_axis=0)
        col_mat[:, k * TILE : (k + 1) * TILE] = ring.T.astype(BF16)
    place_w = lax.broadcasted_iota(jnp.int32, (TILE, 512), 0)
    place_l = lax.broadcasted_iota(jnp.int32, (TILE, 512), 1)
    picker = jnp.where(
        jnp.logical_and(place_l == lax.div(place_w, 16) * STRIP + lax.rem(place_w, 16), place_w < 48),
        1.0,
        0.0,
    ).astype(BF16)
    stacked = []
    for k in range(NB):
        taps = rows_ref[k : k + 1, :].astype(BF16).astype(F32)
        base = pltpu.roll(jnp.concatenate([taps, pad], 1), 4, 1)
        stacked.append(pltpu.roll(jnp.broadcast_to(base, (16, TILE)), 0, 1, stride=1, stride_axis=0))
    spread = jnp.dot(
        jnp.concatenate(stacked, 0).astype(BF16), picker, preferred_element_type=F32
    )
    first = jnp.zeros((16, 512), F32)
    for k in range(NB):
        first = first + pltpu.roll(spread[16 * k : 16 * k + 16], 16 * k, 1)
    first = jnp.concatenate([first, jnp.zeros((16, 1024), F32)], 1)
    for u in range(8):
        row_mat[16 * u : 16 * u + 16, :] = pltpu.roll(first, STRIP * u, 1)[:, :KROWS].astype(BF16)


def column_pass(picture, col_mat, mid):
    mid[0] = jnp.zeros((NB, 16, IMG), BF16)
    mid[65] = jnp.zeros((NB, 16, IMG), BF16)
    near = lax.broadcasted_iota(jnp.int32, (IMG, TILE), 1) < 64

    def one(j, _):
        here = picture[:, lanes_of(j)]
        after = picture[:, lanes_of(jnp.minimum(j + 1, 7))]
        before = picture[:, lanes_of(jnp.maximum(j - 1, 0))]
        zero = jnp.zeros_like(here)
        after = jnp.where(jnp.broadcast_to(j < 7, near.shape), after, zero)
        before = jnp.where(jnp.broadcast_to(j > 0, near.shape), before, zero)
        lhs = jnp.concatenate([here, jnp.where(near, after, before)], 1)
        for k in range(0, NB, 2):
            count = min(2, NB - k)
            got = jnp.dot(
                lhs, col_mat[:, k * TILE : (k + count) * TILE], preferred_element_type=F32
            ).astype(BF16)
            for t in range(count):
                mid[1:65, k + t, :, lanes_of(j)] = got[:, t * TILE : (t + 1) * TILE].reshape(64, 16, TILE)
        return 0

    lax.fori_loop(0, 8, one, 0)


def build_detection(detect_ref, pack_mat, smooth_mat, filter_mat):
    row = lax.broadcasted_iota(jnp.int32, (IMG, 2 * TILE), 0)
    lane = lax.broadcasted_iota(jnp.int32, (IMG, 2 * TILE), 1)
    block, inner = lax.div(row, TILE), lax.rem(row, TILE)
    last = jnp.logical_and(inner >= 112, lane == block * 16 + inner - 112)
    first = jnp.logical_and(inner < 16, lane == TILE + block * 16 + inner)
    pack_mat[...] = jnp.where(jnp.logical_or(last, first), 1.0, 0.0).astype(BF16)
    taps = detect_ref[...].astype(BF16).astype(F32)
    taps = jnp.concatenate(
        [taps, jnp.zeros((1, TILE - DTAPS), F32), jnp.zeros((1, TILE), F32)], 1
    )

    def ring(shift):
        base = jnp.broadcast_to(pltpu.roll(taps, shift, 1), (TILE, 2 * TILE))
        return pltpu.roll(base, 0, 1, stride=1, stride_axis=0)

    table = ring(2 * TILE - 15)
    table = jnp.concatenate([table[:, :TILE].T, table[:, TILE:].T], 0).astype(BF16)
    smooth_mat[0:TILE] = table[0:TILE]
    for b in range(8):
        smooth_mat[TILE + 16 * b : TILE + 16 * b + 16] = table[240:256]
        smooth_mat[2 * TILE + 16 * b : 2 * TILE + 16 * b + 16] = table[128:144]
    filter_mat[...] = ring(1)[:, :160].astype(BF16)


def coadd_kernel(
    picture_in,
    variance_in,
    planes_ref,
    sky_ref,
    rows_ref,
    cols_ref,
    coeff_ref,
    detect_ref,
    difference_out,
    detection_out,
    picture,
    variance,
    col_keep,
    row_keep,
    col_mat,
    row_mat,
    mid,
    matched,
    w_send,
    w_recv,
    m_send,
    m_recv,
    p_send,
    p_recv,
    numer_own,
    denom_own,
    t_all,
    q_send,
    q_recv,
    flat_ref,
    d_out,
    pack_mat,
    smooth_mat,
    filter_mat,
    natural,
    e_send,
    e_recv,
    smooth,
    power,
    b_recv,
    detection,
    load_sem,
    out_sem,
    send_sem,
    w_sem,
    m_sem,
    p_sem,
    t_sem,
    q_sem,
    x_sem,
    e_sem,
    b_sem,
):
    own = lax.axis_index("sky")
    band = lax.axis_index("band")
    barrier = pltpu.get_barrier_semaphore()
    for half in range(2):
        klass, slot = place(half)
        for d in range(1, 8):
            peer = device_of(half, lax.rem(klass + d, 8), slot)
            pl.semaphore_signal(barrier, inc=1, device_id=(peer, band), device_id_type=MESH)
    mirror = turned_column(own)
    for step in (1, 31):
        for peer in (
            lax.rem(own + step, 32),
            lax.rem(mirror + step, 32),
            turned_column(lax.rem(own + step, 32)),
        ):
            pl.semaphore_signal(barrier, inc=1, device_id=(peer, band), device_id_type=MESH)
    for step in range(1, 4):
        pl.semaphore_signal(
            barrier, inc=1, device_id=(own, lax.rem(band + step, 4)), device_id_type=MESH
        )

    @pl.when(mirror != own)
    def _():
        pl.semaphore_signal(barrier, inc=1, device_id=(mirror, band), device_id_type=MESH)

    load_variance = pltpu.make_async_copy(variance_in, variance, load_sem.at[0])
    load_picture = pltpu.make_async_copy(picture_in, picture, load_sem.at[1])
    load_variance.start()
    load_picture.start()
    start = sky_ref[own, band, 0]
    col_keep[...] = bit_lanes(planes_ref, 0)
    row_keep[...] = bit_lanes(planes_ref, 1)
    load_variance.wait()
    pl.semaphore_wait(barrier, jnp.where(mirror != own, 24, 23))

    def send(src, dst, sem_send, sem_recv, device, to_band=None):
        pltpu.make_async_remote_copy(
            src_ref=src,
            dst_ref=dst,
            send_sem=sem_send,
            recv_sem=sem_recv,
            device_id=(device, band if to_band is None else to_band),
            device_id_type=MESH,
        ).start()

    def wait_for(ref, sem):
        pltpu.make_async_copy(ref, ref, sem).wait()

    def to_group(step, src, dst, sem_send, sem_recv):
        half, block = row_block(step)
        klass, slot = place(half)
        for d in range(1, 8):
            peer = device_of(half, lax.rem(klass + d, 8), slot)
            send(src.at[d, rows_of(block)], dst.at[d, rows_of(block)], sem_send, sem_recv.at[step], peer)

    def stage_weight(step, _):
        half, block = row_block(step)
        klass, slot = place(half)
        flat_ref[...] = jnp.broadcast_to(row_keep[0:1, lanes_of(block)], (TILE, TILE)).T

        def part(r, _):
            at = pl.ds(pl.multiple_of(block * TILE + r * 32, 32), 32)
            flat = flat_ref[pl.ds(pl.multiple_of(r * 32, 32), 32), :]
            tiles = []
            for c in range(8):
                keep = flat * col_keep[0:1, c * TILE : (c + 1) * TILE]
                tiles.append(
                    (variance[at, c * TILE : (c + 1) * TILE].astype(F32) * keep).astype(BF16)
                )
            for d, tile in enumerate(turned(tiles, klass - start + 32)):
                w_send[d, at, :] = tile
            return 0

        lax.fori_loop(0, 4, part, 0)
        to_group(step, w_send, w_recv, send_sem.at[0], w_sem)
        return 0

    lax.fori_loop(0, NCHUNK, stage_weight, 0)
    build_taps(cols_ref, rows_ref, coeff_ref, col_mat, row_mat)
    build_detection(detect_ref, pack_mat, smooth_mat, filter_mat)
    load_picture.wait()
    column_pass(picture, col_mat, mid)

    def stage_matched(step, _):
        half, block = row_block(step)
        klass, slot = place(half)
        window = mid[pl.ds(block * 8, 10)].reshape(KROWS, IMG)
        matched[...] = jnp.dot(row_mat[...], window, preferred_element_type=F32).astype(BF16)

        def part(r, _):
            at = pl.ds(pl.multiple_of(block * TILE + r * 32, 32), 32)
            inner = pl.ds(pl.multiple_of(r * 32, 32), 32)
            tiles = [matched[inner, c * TILE : (c + 1) * TILE] for c in range(8)]
            for d, tile in enumerate(turned(tiles, klass - start + 32)):
                m_send[d, at, :] = tile
            return 0

        lax.fori_loop(0, 4, part, 0)
        to_group(step, m_send, m_recv, send_sem.at[1], m_sem)
        return 0

    lax.fori_loop(0, NCHUNK, stage_matched, 0)

    def column_slot(exposure, klass):
        begin = sky_ref[exposure, band, 0]
        c = jnp.bitwise_and(klass - begin + 32, 7)
        return lax.shift_right_logical(jnp.bitwise_and(begin + c, 31), 3)

    def reduce_group(step, _):
        half, block = row_block(step)
        klass, slot = place(half)
        wait_for(w_recv.at[pl.ds(1, 7), rows_of(block)], w_sem.at[step])
        wait_for(m_recv.at[pl.ds(1, 7), rows_of(block)], m_sem.at[step])
        rel = []
        for d in range(8):
            source = device_of(half, lax.rem(klass - d + 8, 8), slot)
            rel.append(jnp.full((32, TILE), jnp.bitwise_and(column_slot(source, klass) - slot + 4, 3), jnp.int32))

        def part(r, _):
            at = pl.ds(pl.multiple_of(block * TILE + r * 32, 32), 32)
            inner = pl.ds(pl.multiple_of(r * 32, 32), 32)
            numer = [jnp.zeros((32, TILE), F32) for _ in range(4)]
            denom = [jnp.zeros((32, TILE), F32) for _ in range(4)]
            for d in range(8):
                w = (w_recv if d else w_send)[d, at, :].astype(F32)
                wm = w * (m_recv if d else m_send)[d, at, :].astype(F32)
                for t in range(4):
                    hit = rel[d] == t
                    numer[t] = numer[t] + jnp.where(hit, wm, 0.0)
                    denom[t] = denom[t] + jnp.where(hit, w, 0.0)
            numer_own[at, :] = numer[0]
            denom_own[at, :] = denom[0]
            for t in range(1, 4):
                p_send[t, block, 0, inner, :] = numer[t].astype(BF16)
                p_send[t, block, 1, inner, :] = denom[t].astype(BF16)
            return 0

        lax.fori_loop(0, 4, part, 0)
        for t in range(1, 4):
            peer = device_of(half, klass, lax.rem(slot + t, 4))
            send(p_send.at[t, block], p_recv.at[t, block], send_sem.at[2], p_sem.at[step], peer)
        return 0

    lax.fori_loop(0, NCHUNK, reduce_group, 0)

    def make_template(step, _):
        half, block = row_block(step)
        klass, slot = place(half)
        wait_for(p_recv.at[pl.ds(1, 3), block], p_sem.at[step])
        numer = numer_own[rows_of(block), :]
        denom = denom_own[rows_of(block), :]
        for t in range(1, 4):
            numer = numer + p_recv[t, block, 0].astype(F32)
            denom = denom + p_recv[t, block, 1].astype(F32)
        t_all[0, rows_of(block), :] = (numer / jnp.maximum(denom, 1.0)).astype(BF16)
        for t in range(1, 4):
            peer = device_of(half, klass, lax.rem(slot + t, 4))
            send(t_all.at[0, rows_of(block)], t_all.at[t, rows_of(block)], send_sem.at[3], t_sem.at[step], peer)
        return 0

    lax.fori_loop(0, NCHUNK, make_template, 0)
    lower = t_all.at[0, pl.ds(512, 512)]

    @pl.when(mirror != own)
    def _():
        send(lower, natural, send_sem.at[5], x_sem, mirror)

    @pl.when(mirror == own)
    def _():
        pltpu.make_async_copy(lower, natural, x_sem).start()

    for half in range(2):
        column = mirror if half else own
        wide = jnp.concatenate(
            [t_all[0, half * 512 + 64 * b : half * 512 + 64 * b + 64, :] for b in range(8)], 1
        )
        packed = jnp.dot(wide, pack_mat[...], preferred_element_type=F32).astype(BF16)
        for side in range(2):
            e_send[half, side] = packed[:, side * TILE : (side + 1) * TILE]
            peer = lax.rem(column + (31 if side else 1), 32)
            send(e_send.at[half, side], e_recv.at[half, side], send_sem.at[6], e_sem, peer)

    def pick_templates(step, _):
        half, block = row_block(step)
        klass, slot = place(half)
        wait_for(t_all.at[pl.ds(1, 3), rows_of(block)], t_sem.at[step])
        for d in range(8):
            target = device_of(half, lax.rem(klass + d, 8), slot)
            rel = jnp.full((TILE, TILE), jnp.bitwise_and(slot - column_slot(target, klass) + 4, 3), jnp.int32)
            value = t_all[0, rows_of(block), :]
            for t in range(1, 4):
                value = jnp.where(rel == t, t_all[t, rows_of(block), :], value)
            q_send[d, rows_of(block), :] = value
        to_group(step, q_send, q_recv, send_sem.at[4], q_sem)
        return 0

    lax.fori_loop(0, NCHUNK, pick_templates, 0)
    wait_for(natural, x_sem)
    wait_for(e_recv, e_sem)
    smooth[0:16] = jnp.zeros((16, TILE), BF16)
    smooth[IMG + 16 : IMG + 32] = jnp.zeros((16, TILE), BF16)
    group = lax.div(lax.broadcasted_iota(jnp.int32, (64, TILE), 1), 16)
    for quarter in range(4):
        half = quarter // 2
        pieces = []
        for b in range(4 * (quarter % 2), 4 * (quarter % 2) + 4):
            here = natural[64 * b : 64 * b + 64, :] if half else t_all[0, 64 * b : 64 * b + 64, :]
            zero = jnp.zeros((64, TILE), BF16)
            left = jnp.where(group == b, e_recv[half, 0], zero)
            right = jnp.where(group == b, e_recv[half, 1], zero)
            pieces.append(jnp.concatenate([here, left, right], 1))
        got = jnp.dot(jnp.concatenate(pieces, 0), smooth_mat[...], preferred_element_type=F32)
        smooth[16 + 256 * quarter : 272 + 256 * quarter] = got.astype(BF16)
    for i in range(8):
        got = jnp.dot(
            filter_mat[...], smooth[TILE * i : TILE * i + 160], preferred_element_type=F32
        )
        power[TILE * i : TILE * i + TILE] = got * got
    for t in range(1, 4):
        target = lax.rem(band + t, 4)
        send(power.at[quarter_of(target)], b_recv.at[t - 1], send_sem.at[7], b_sem, own, target)

    def subtract(step, _):
        half, block = row_block(step)
        klass, slot = place(half)
        wait_for(q_recv.at[pl.ds(1, 7), rows_of(block)], q_sem.at[step])

        def part(r, _):
            at = pl.ds(pl.multiple_of(block * TILE + r * 32, 32), 32)
            tiles = []
            for i in range(8):
                d = (8 - i) % 8
                m = m_send[i, at, :].astype(F32)
                q = (q_recv if d else q_send)[d, at, :].astype(F32)
                tiles.append((m - q).astype(BF16))
            for c, tile in enumerate(turned(tiles, start - klass + 32)):
                d_out[at, c * TILE : (c + 1) * TILE] = tile
            return 0

        lax.fori_loop(0, 4, part, 0)
        pltpu.make_async_copy(d_out.at[rows_of(block)], difference_out.at[rows_of(block)], out_sem).start()
        return 0

    lax.fori_loop(0, NCHUNK, subtract, 0)
    wait_for(b_recv, b_sem)
    detection[...] = power[quarter_of(band), :] + b_recv[0] + b_recv[1] + b_recv[2]
    save = pltpu.make_async_copy(detection, detection_out, load_sem.at[2])
    save.start()
    save.wait()
    wait_for(d_out, out_sem)
    wait_for(w_send.at[pl.ds(1, 7)], send_sem.at[0])
    wait_for(m_send.at[pl.ds(1, 7)], send_sem.at[1])
    wait_for(p_send.at[pl.ds(1, 3)], send_sem.at[2])
    wait_for(t_all.at[pl.ds(1, 3)], send_sem.at[3])
    wait_for(q_send.at[pl.ds(1, 7)], send_sem.at[4])

    @pl.when(mirror != own)
    def _():
        wait_for(natural, send_sem.at[5])

    wait_for(e_send, send_sem.at[6])
    wait_for(b_recv, send_sem.at[7])


def coadd(picture, variance, planes, sky_columns, basis_rows, basis_cols, coeffs, detect_taps):
    vmem = pl.BlockSpec(memory_space=pltpu.VMEM)
    smem = pl.BlockSpec(memory_space=pltpu.SMEM)
    anyw = pl.BlockSpec(memory_space=pl.ANY)
    tiles = pltpu.VMEM((8, IMG, TILE), BF16)
    parts = pltpu.VMEM((4, NCHUNK, 2, TILE, TILE), BF16)
    return pl.pallas_call(
        coadd_kernel,
        out_shape=(
            jax.ShapeDtypeStruct((IMG, IMG), BF16),
            jax.ShapeDtypeStruct((IMG // 4, TILE), F32),
        ),
        in_specs=[anyw, anyw, smem, smem, vmem, vmem, smem, vmem],
        out_specs=(anyw, anyw),
        scratch_shapes=[
            pltpu.VMEM((IMG, IMG), BF16),
            pltpu.VMEM((IMG, IMG), BF16),
            pltpu.VMEM((8, IMG), F32),
            pltpu.VMEM((8, IMG), F32),
            pltpu.VMEM((2 * TILE, NB * TILE), BF16),
            pltpu.VMEM((TILE, KROWS), BF16),
            pltpu.VMEM((66, NB, 16, IMG), BF16),
            pltpu.VMEM((TILE, IMG), BF16),
            tiles,
            tiles,
            tiles,
            tiles,
            parts,
            parts,
            pltpu.VMEM((IMG, TILE), F32),
            pltpu.VMEM((IMG, TILE), F32),
            pltpu.VMEM((4, IMG, TILE), BF16),
            tiles,
            tiles,
            pltpu.VMEM((TILE, TILE), F32),
            pltpu.VMEM((IMG, IMG), BF16),
            pltpu.VMEM((IMG, 2 * TILE), BF16),
            pltpu.VMEM((3 * TILE, TILE), BF16),
            pltpu.VMEM((TILE, 160), BF16),
            pltpu.VMEM((512, TILE), BF16),
            pltpu.VMEM((2, 2, 64, TILE), BF16),
            pltpu.VMEM((2, 2, 64, TILE), BF16),
            pltpu.VMEM((IMG + 32, TILE), BF16),
            pltpu.VMEM((IMG, TILE), F32),
            pltpu.VMEM((3, IMG // 4, TILE), F32),
            pltpu.VMEM((IMG // 4, TILE), F32),
            pltpu.SemaphoreType.DMA((3,)),
            pltpu.SemaphoreType.DMA,
            pltpu.SemaphoreType.DMA((8,)),
            pltpu.SemaphoreType.DMA((NCHUNK,)),
            pltpu.SemaphoreType.DMA((NCHUNK,)),
            pltpu.SemaphoreType.DMA((NCHUNK,)),
            pltpu.SemaphoreType.DMA((NCHUNK,)),
            pltpu.SemaphoreType.DMA((NCHUNK,)),
            pltpu.SemaphoreType.DMA,
            pltpu.SemaphoreType.DMA,
            pltpu.SemaphoreType.DMA,
        ],
        compiler_params=pltpu.CompilerParams(
            collective_id=0, has_side_effects=True, vmem_limit_bytes=60 << 20
        ),
        name="coadd",
    )(picture, variance, planes, sky_columns, basis_rows, basis_cols, coeffs, detect_taps)


def body(
    exposures,
    inv_variance,
    mask_planes,
    sky_columns,
    basis_rows,
    basis_cols,
    match_coeffs,
    detect_taps,
):
    difference, detection = coadd(
        exposures[0, 0],
        inv_variance[0, 0],
        mask_planes[0, 0],
        sky_columns,
        basis_rows,
        basis_cols,
        match_coeffs[0],
        detect_taps,
    )
    return (difference[None, None], detection)


def solution(mesh):
    in_specs = (
        P("sky", "band", None, None),
        P("sky", "band", None, None),
        P("sky", "band", None, None),
        P(),
        P(),
        P(),
        P("sky", "band", None),
        P("band", None),
    )
    out_specs = (P("sky", "band", None, None), P("band", "sky"))
    return jax.shard_map(body, mesh=mesh, in_specs=in_specs, out_specs=out_specs, check_vma=False)
```

```python
import jax
import jax.numpy as jnp
from jax import lax
from jax.experimental import pallas as pl
from jax.experimental.pallas import tpu as pltpu
from jax.sharding import PartitionSpec as P

TILE = 128
NB = 9
TAPS = 25
DTAPS = 31
IMG = 1024
HALO = 12
STRIP = NB * 16
KROWS = 10 * STRIP
CHUNK = 128
STEPS = 512 // CHUNK
MESH = pl.DeviceIdType.MESH
F32 = jnp.float32
BF16 = jnp.bfloat16


def rows_of(block):
    return pl.ds(pl.multiple_of(block * TILE, TILE), TILE)


def quarter_of(block):
    return pl.ds(pl.multiple_of(block * 256, 256), 256)


def lanes_of(block):
    return pl.ds(pl.multiple_of(block * TILE, TILE), TILE)


def device_of(half, klass, slot):
    if half == 0:
        return 8 * slot + klass
    return 8 * lax.div(klass, 2) + 2 * slot + lax.rem(klass, 2)


def place(half):
    own = lax.axis_index("sky")
    y, rest = lax.div(own, 8), lax.rem(own, 8)
    z, core = lax.div(rest, 2), lax.rem(rest, 2)
    return (2 * y + core, z) if half else (rest, y)


def turned_column(column):
    y, rest = lax.div(column, 8), lax.rem(column, 8)
    return 8 * lax.div(rest, 2) + 2 * y + lax.rem(rest, 2)


def chunk_of(half, step):
    return pl.ds(pl.multiple_of(half * 512 + step * CHUNK, CHUNK), CHUNK)


def strip_of(half, step, part):
    return pl.ds(pl.multiple_of(half * 512 + step * CHUNK + part * 32, 32), 32)


def turned(tiles, amount):
    for bit in (1, 2, 4):
        take = jnp.bitwise_and(jnp.full(tiles[0].shape, amount, jnp.int32), bit) != 0
        tiles = [jnp.where(take, tiles[(i + bit) % 8], tiles[i]) for i in range(8)]
    return tiles


def bit_lanes(planes_ref, plane):
    lane = lax.broadcasted_iota(jnp.int32, (8, IMG), 1)
    word = jnp.zeros((8, IMG), jnp.int32)
    first = jnp.zeros((8, IMG), jnp.int32)
    for index in range(35):
        inside = lane >= 30 * index
        word = jnp.where(inside, planes_ref[plane, index], word)
        first = jnp.where(inside, 30 * index, first)
    bit = jnp.bitwise_and(lax.shift_right_logical(word, lane - first), 1)
    return (1 - bit).astype(F32)


def build_taps(cols_ref, rows_ref, coeff_ref, col_mat, row_mat):
    pad = jnp.zeros((1, TILE - TAPS), F32)
    far = jnp.zeros((1, TILE), F32)
    for k in range(NB):
        taps = (cols_ref[k : k + 1, :] * coeff_ref[0, k]).astype(BF16).astype(F32)
        base = pltpu.roll(jnp.concatenate([taps, pad, far], 1), 2 * TILE - HALO, 1)
        ring = pltpu.roll(jnp.broadcast_to(base, (TILE, 2 * TILE)), 0, 1, stride=1, stride_axis=0)
        col_mat[:, k * TILE : (k + 1) * TILE] = ring.T.astype(BF16)
    place_w = lax.broadcasted_iota(jnp.int32, (TILE, 512), 0)
    place_l = lax.broadcasted_iota(jnp.int32, (TILE, 512), 1)
    picker = jnp.where(
        jnp.logical_and(place_l == lax.div(place_w, 16) * STRIP + lax.rem(place_w, 16), place_w < 48),
        1.0,
        0.0,
    ).astype(BF16)
    stacked = []
    for k in range(NB):
        taps = rows_ref[k : k + 1, :].astype(BF16).astype(F32)
        base = pltpu.roll(jnp.concatenate([taps, pad], 1), 4, 1)
        stacked.append(pltpu.roll(jnp.broadcast_to(base, (16, TILE)), 0, 1, stride=1, stride_axis=0))
    spread = jnp.dot(
        jnp.concatenate(stacked, 0).astype(BF16), picker, preferred_element_type=F32
    )
    first = jnp.zeros((16, 512), F32)
    for k in range(NB):
        first = first + pltpu.roll(spread[16 * k : 16 * k + 16], 16 * k, 1)
    first = jnp.concatenate([first, jnp.zeros((16, 1024), F32)], 1)
    for u in range(8):
        row_mat[16 * u : 16 * u + 16, :] = pltpu.roll(first, STRIP * u, 1)[:, :KROWS].astype(BF16)


def column_pass(picture, col_mat, mid):
    mid[0] = jnp.zeros((NB, 16, IMG), BF16)
    mid[65] = jnp.zeros((NB, 16, IMG), BF16)
    near = lax.broadcasted_iota(jnp.int32, (IMG, TILE), 1) < 64

    def one(j, _):
        here = picture[:, lanes_of(j)]
        after = picture[:, lanes_of(jnp.minimum(j + 1, 7))]
        before = picture[:, lanes_of(jnp.maximum(j - 1, 0))]
        zero = jnp.zeros_like(here)
        after = jnp.where(jnp.broadcast_to(j < 7, near.shape), after, zero)
        before = jnp.where(jnp.broadcast_to(j > 0, near.shape), before, zero)
        lhs = jnp.concatenate([here, jnp.where(near, after, before)], 1)
        for k in range(0, NB, 2):
            count = min(2, NB - k)
            got = jnp.dot(
                lhs, col_mat[:, k * TILE : (k + count) * TILE], preferred_element_type=F32
            ).astype(BF16)
            for t in range(count):
                mid[1:65, k + t, :, lanes_of(j)] = got[:, t * TILE : (t + 1) * TILE].reshape(64, 16, TILE)
        return 0

    lax.fori_loop(0, 8, one, 0)


def build_detection(detect_ref, pack_mat, smooth_mat, filter_mat):
    row = lax.broadcasted_iota(jnp.int32, (IMG, 2 * TILE), 0)
    lane = lax.broadcasted_iota(jnp.int32, (IMG, 2 * TILE), 1)
    block, inner = lax.div(row, TILE), lax.rem(row, TILE)
    last = jnp.logical_and(inner >= 112, lane == block * 16 + inner - 112)
    first = jnp.logical_and(inner < 16, lane == TILE + block * 16 + inner)
    pack_mat[...] = jnp.where(jnp.logical_or(last, first), 1.0, 0.0).astype(BF16)
    taps = detect_ref[...].astype(BF16).astype(F32)
    taps = jnp.concatenate(
        [taps, jnp.zeros((1, TILE - DTAPS), F32), jnp.zeros((1, TILE), F32)], 1
    )

    def ring(shift):
        base = jnp.broadcast_to(pltpu.roll(taps, shift, 1), (TILE, 2 * TILE))
        return pltpu.roll(base, 0, 1, stride=1, stride_axis=0)

    table = ring(2 * TILE - 15)
    table = jnp.concatenate([table[:, :TILE].T, table[:, TILE:].T], 0).astype(BF16)
    smooth_mat[0:TILE] = table[0:TILE]
    for b in range(8):
        smooth_mat[TILE + 16 * b : TILE + 16 * b + 16] = table[240:256]
        smooth_mat[2 * TILE + 16 * b : 2 * TILE + 16 * b + 16] = table[128:144]
    filter_mat[...] = ring(1)[:, :160].astype(BF16)


def coadd_kernel(
    picture_in,
    variance_in,
    planes_ref,
    sky_in,
    rows_ref,
    cols_ref,
    coeff_ref,
    detect_ref,
    difference_out,
    detection_out,
    picture,
    variance,
    sky_ref,
    col_keep,
    col_mat,
    row_mat,
    mid,
    matched,
    w_send,
    w_recv,
    m_send,
    m_recv,
    p_send,
    p_recv,
    numer_own,
    denom_own,
    t_all,
    q_send,
    q_recv,
    flat_ref,
    pack_mat,
    smooth_mat,
    filter_mat,
    natural,
    e_send,
    e_recv,
    smooth,
    power,
    b_recv,
    load_sem,
    send_sem,
    w_sem,
    m_sem,
    p_sem,
    t_sem,
    q_sem,
    x_sem,
    e_sem,
    b_sem,
):
    own = lax.axis_index("sky")
    band = lax.axis_index("band")
    barrier = pltpu.get_barrier_semaphore()
    places, group, sources, ring = [], [], [], []
    for half in range(2):
        klass, slot = place(half)
        places.append((klass, slot))
        group.append([device_of(half, lax.rem(klass + d, 8), slot) for d in range(8)])
        sources.append([device_of(half, lax.rem(klass + 8 - d, 8), slot) for d in range(8)])
        ring.append([device_of(half, klass, lax.rem(slot + t, 4)) for t in range(4)])
        for d in range(1, 8):
            pl.semaphore_signal(
                barrier, inc=1, device_id=(group[half][d], band), device_id_type=MESH
            )
    mirror = turned_column(own)
    for step in (1, 31):
        for peer in (
            lax.rem(own + step, 32),
            lax.rem(mirror + step, 32),
            turned_column(lax.rem(own + step, 32)),
        ):
            pl.semaphore_signal(barrier, inc=1, device_id=(peer, band), device_id_type=MESH)
    for step in range(1, 4):
        pl.semaphore_signal(
            barrier, inc=1, device_id=(own, lax.rem(band + step, 4)), device_id_type=MESH
        )

    @pl.when(mirror != own)
    def _():
        pl.semaphore_signal(barrier, inc=1, device_id=(mirror, band), device_id_type=MESH)

    load_sky = pltpu.make_async_copy(sky_in, sky_ref, load_sem.at[2])
    load_variance = pltpu.make_async_copy(variance_in, variance, load_sem.at[0])
    load_picture = pltpu.make_async_copy(picture_in, picture, load_sem.at[1])
    load_sky.start()
    load_variance.start()
    load_picture.start()
    col_keep[...] = bit_lanes(planes_ref, 0)
    row_keep = bit_lanes(planes_ref, 1)
    for i in range(8):
        flat_ref[i * TILE : (i + 1) * TILE] = jnp.broadcast_to(
            row_keep[0:1, i * TILE : (i + 1) * TILE], (TILE, TILE)
        ).T
    load_sky.wait()
    start = sky_ref[band, 0, own]
    turn = [places[half][0] - start + 32 for half in range(2)]
    load_variance.wait()
    pl.semaphore_wait(barrier, jnp.where(mirror != own, 24, 23))

    def send(src, dst, sem_send, sem_recv, device, to_band=None):
        pltpu.make_async_remote_copy(
            src_ref=src,
            dst_ref=dst,
            send_sem=sem_send,
            recv_sem=sem_recv,
            device_id=(device, band if to_band is None else to_band),
            device_id_type=MESH,
        ).start()

    def wait_for(ref, sem):
        pltpu.make_async_copy(ref, ref, sem).wait()

    def to_group(half, step, src, dst, sem_send, sem_recv):
        rows = chunk_of(half, step)
        for d in range(1, 8):
            send(
                src.at[d, rows], dst.at[d, rows], sem_send, sem_recv.at[half, step], group[half][d]
            )

    def stage_weight(step, _):
        for half in range(2):

            def part(r, _):
                at = strip_of(half, step, r)
                flat = flat_ref[at, :]
                tiles = []
                for c in range(8):
                    keep = flat * col_keep[0:1, c * TILE : (c + 1) * TILE]
                    tiles.append(
                        (variance[at, c * TILE : (c + 1) * TILE].astype(F32) * keep).astype(BF16)
                    )
                for d, tile in enumerate(turned(tiles, turn[half])):
                    w_send[d, at, :] = tile
                return 0

            lax.fori_loop(0, CHUNK // 32, part, 0)
            to_group(half, step, w_send, w_recv, send_sem.at[0], w_sem)
        return 0

    lax.fori_loop(0, STEPS, stage_weight, 0)
    build_taps(cols_ref, rows_ref, coeff_ref, col_mat, row_mat)
    build_detection(detect_ref, pack_mat, smooth_mat, filter_mat)
    load_picture.wait()
    column_pass(picture, col_mat, mid)

    def stage_matched(step, _):
        for half in range(2):

            def block(i, _):
                first = half * 32 + step * (CHUNK // 16) + i * 8
                window = mid[pl.ds(first, 10)].reshape(KROWS, IMG)
                matched[...] = jnp.dot(
                    row_mat[...], window, preferred_element_type=F32
                ).astype(BF16)

                def part(r, _):
                    at = strip_of(half, step, i * 4 + r)
                    inner = pl.ds(pl.multiple_of(r * 32, 32), 32)
                    tiles = [matched[inner, c * TILE : (c + 1) * TILE] for c in range(8)]
                    for d, tile in enumerate(turned(tiles, turn[half])):
                        m_send[d, at, :] = tile
                    return 0

                lax.fori_loop(0, 4, part, 0)
                return 0

            lax.fori_loop(0, CHUNK // TILE, block, 0)
            to_group(half, step, m_send, m_recv, send_sem.at[1], m_sem)
        return 0

    lax.fori_loop(0, STEPS, stage_matched, 0)

    def column_slot(exposure, klass):
        begin = sky_ref[band, 0, exposure]
        c = jnp.bitwise_and(klass - begin + 32, 7)
        return lax.shift_right_logical(jnp.bitwise_and(begin + c, 31), 3)

    def reduce_group(step, _):
        for half in range(2):
            klass, slot = places[half]
            rows = chunk_of(half, step)
            piece = half * STEPS + step
            wait_for(w_recv.at[pl.ds(1, 7), rows], w_sem.at[half, step])
            wait_for(m_recv.at[pl.ds(1, 7), rows], m_sem.at[half, step])
            rel = [
                jnp.full(
                    (32, TILE),
                    jnp.bitwise_and(column_slot(sources[half][d], klass) - slot + 4, 3),
                    jnp.int32,
                )
                for d in range(8)
            ]

            def part(r, _):
                at = strip_of(half, step, r)
                inner = pl.ds(pl.multiple_of(r * 32, 32), 32)
                numer = [jnp.zeros((32, TILE), F32) for _ in range(4)]
                denom = [jnp.zeros((32, TILE), F32) for _ in range(4)]
                for d in range(8):
                    w = (w_recv if d else w_send)[d, at, :].astype(F32)
                    wm = w * (m_recv if d else m_send)[d, at, :].astype(F32)
                    for t in range(4):
                        hit = rel[d] == t
                        numer[t] = numer[t] + jnp.where(hit, wm, 0.0)
                        denom[t] = denom[t] + jnp.where(hit, w, 0.0)
                numer_own[at, :] = numer[0]
                denom_own[at, :] = denom[0]
                for t in range(1, 4):
                    p_send[t, piece, 0, inner, :] = numer[t].astype(BF16)
                    p_send[t, piece, 1, inner, :] = denom[t].astype(BF16)
                return 0

            lax.fori_loop(0, CHUNK // 32, part, 0)
            for t in range(1, 4):
                send(
                    p_send.at[t, piece],
                    p_recv.at[t, piece],
                    send_sem.at[2],
                    p_sem.at[half, step],
                    ring[half][t],
                )
        return 0

    lax.fori_loop(0, STEPS, reduce_group, 0)

    def make_template(step, _):
        for half in range(2):
            rows = chunk_of(half, step)
            piece = half * STEPS + step
            wait_for(p_recv.at[pl.ds(1, 3), piece], p_sem.at[half, step])

            def part(r, _):
                at = strip_of(half, step, r)
                inner = pl.ds(pl.multiple_of(r * 32, 32), 32)
                numer = numer_own[at, :]
                denom = denom_own[at, :]
                for t in range(1, 4):
                    numer = numer + p_recv[t, piece, 0, inner, :].astype(F32)
                    denom = denom + p_recv[t, piece, 1, inner, :].astype(F32)
                t_all[0, at, :] = (numer / jnp.maximum(denom, 1.0)).astype(BF16)
                return 0

            lax.fori_loop(0, CHUNK // 32, part, 0)
            for t in range(1, 4):
                send(
                    t_all.at[0, rows],
                    t_all.at[t, rows],
                    send_sem.at[3],
                    t_sem.at[half, step],
                    ring[half][t],
                )
        return 0

    lax.fori_loop(0, STEPS, make_template, 0)
    lower = t_all.at[0, pl.ds(512, 512)]

    @pl.when(mirror != own)
    def _():
        send(lower, natural, send_sem.at[5], x_sem, mirror)

    @pl.when(mirror == own)
    def _():
        pltpu.make_async_copy(lower, natural, x_sem).start()

    for half in range(2):
        column = mirror if half else own
        wide = jnp.concatenate(
            [t_all[0, half * 512 + 64 * b : half * 512 + 64 * b + 64, :] for b in range(8)], 1
        )
        packed = jnp.dot(wide, pack_mat[...], preferred_element_type=F32).astype(BF16)
        for side in range(2):
            e_send[half, side] = packed[:, side * TILE : (side + 1) * TILE]
            peer = lax.rem(column + (31 if side else 1), 32)
            send(e_send.at[half, side], e_recv.at[half, side], send_sem.at[6], e_sem, peer)

    def pick_templates(step, _):
        for half in range(2):
            klass, slot = places[half]
            rows = chunk_of(half, step)
            wait_for(t_all.at[pl.ds(1, 3), rows], t_sem.at[half, step])
            rel = [
                jnp.full(
                    (32, TILE),
                    jnp.bitwise_and(slot - column_slot(group[half][d], klass) + 4, 3),
                    jnp.int32,
                )
                for d in range(8)
            ]

            def part(r, _):
                at = strip_of(half, step, r)
                values = [t_all[t, at, :] for t in range(4)]
                for d in range(8):
                    value = values[0]
                    for t in range(1, 4):
                        value = jnp.where(rel[d] == t, values[t], value)
                    q_send[d, at, :] = value
                return 0

            lax.fori_loop(0, CHUNK // 32, part, 0)
            to_group(half, step, q_send, q_recv, send_sem.at[4], q_sem)
        return 0

    lax.fori_loop(0, STEPS, pick_templates, 0)
    wait_for(natural, x_sem)
    wait_for(e_recv, e_sem)
    smooth[0:16] = jnp.zeros((16, TILE), BF16)
    smooth[IMG + 16 : IMG + 32] = jnp.zeros((16, TILE), BF16)
    lane_group = lax.div(lax.broadcasted_iota(jnp.int32, (64, TILE), 1), 16)
    for quarter in range(4):
        half = quarter // 2
        pieces = []
        for b in range(4 * (quarter % 2), 4 * (quarter % 2) + 4):
            here = natural[64 * b : 64 * b + 64, :] if half else t_all[0, 64 * b : 64 * b + 64, :]
            zero = jnp.zeros((64, TILE), BF16)
            left = jnp.where(lane_group == b, e_recv[half, 0], zero)
            right = jnp.where(lane_group == b, e_recv[half, 1], zero)
            pieces.append(jnp.concatenate([here, left, right], 1))
        got = jnp.dot(jnp.concatenate(pieces, 0), smooth_mat[...], preferred_element_type=F32)
        smooth[16 + 256 * quarter : 272 + 256 * quarter] = got.astype(BF16)
    for i in range(8):
        got = jnp.dot(
            filter_mat[...], smooth[TILE * i : TILE * i + 160], preferred_element_type=F32
        )
        power[TILE * i : TILE * i + TILE] = got * got
    for t in range(1, 4):
        target = lax.rem(band + t, 4)
        send(power.at[quarter_of(target)], b_recv.at[t - 1], send_sem.at[7], b_sem, own, target)

    def subtract(step, _):
        for half in range(2):
            wait_for(q_recv.at[pl.ds(1, 7), chunk_of(half, step)], q_sem.at[half, step])

            def part(r, _):
                at = strip_of(half, step, r)
                tiles = []
                for i in range(8):
                    d = (8 - i) % 8
                    m = m_send[i, at, :].astype(F32)
                    q = (q_recv if d else q_send)[d, at, :].astype(F32)
                    tiles.append((m - q).astype(BF16))
                for c, tile in enumerate(turned(tiles, 64 - turn[half])):
                    difference_out[at, c * TILE : (c + 1) * TILE] = tile
                return 0

            lax.fori_loop(0, CHUNK // 32, part, 0)
        return 0

    lax.fori_loop(0, STEPS, subtract, 0)
    wait_for(b_recv, b_sem)
    detection_out[...] = power[quarter_of(band), :] + b_recv[0] + b_recv[1] + b_recv[2]
    wait_for(w_send.at[pl.ds(1, 7)], send_sem.at[0])
    wait_for(m_send.at[pl.ds(1, 7)], send_sem.at[1])
    wait_for(p_send.at[pl.ds(1, 3)], send_sem.at[2])
    wait_for(t_all.at[pl.ds(1, 3)], send_sem.at[3])
    wait_for(q_send.at[pl.ds(1, 7)], send_sem.at[4])

    @pl.when(mirror != own)
    def _():
        wait_for(natural, send_sem.at[5])

    wait_for(e_send, send_sem.at[6])
    wait_for(b_recv, send_sem.at[7])


def coadd(picture, variance, planes, sky_columns, basis_rows, basis_cols, coeffs, detect_taps):
    vmem = pl.BlockSpec(memory_space=pltpu.VMEM)
    smem = pl.BlockSpec(memory_space=pltpu.SMEM)
    anyw = pl.BlockSpec(memory_space=pl.ANY)
    tiles = pltpu.VMEM((8, IMG, TILE), BF16)
    parts = pltpu.VMEM((4, 2 * STEPS, 2, CHUNK, TILE), BF16)
    arrivals = pltpu.SemaphoreType.DMA((2, STEPS))
    return pl.pallas_call(
        coadd_kernel,
        out_shape=(pltpu.VMEM((IMG, IMG), BF16), pltpu.VMEM((IMG // 4, TILE), F32)),
        in_specs=[anyw, anyw, smem, anyw, vmem, vmem, smem, vmem],
        out_specs=(vmem, vmem),
        scratch_shapes=[
            pltpu.VMEM((IMG, IMG), BF16),
            pltpu.VMEM((IMG, IMG), BF16),
            pltpu.SMEM((4, 8, 32), jnp.int32),
            pltpu.VMEM((8, IMG), F32),
            pltpu.VMEM((2 * TILE, NB * TILE), BF16),
            pltpu.VMEM((TILE, KROWS), BF16),
            pltpu.VMEM((66, NB, 16, IMG), BF16),
            pltpu.VMEM((TILE, IMG), BF16),
            tiles,
            tiles,
            tiles,
            tiles,
            parts,
            parts,
            pltpu.VMEM((IMG, TILE), F32),
            pltpu.VMEM((IMG, TILE), F32),
            pltpu.VMEM((4, IMG, TILE), BF16),
            tiles,
            tiles,
            pltpu.VMEM((IMG, TILE), F32),
            pltpu.VMEM((IMG, 2 * TILE), BF16),
            pltpu.VMEM((3 * TILE, TILE), BF16),
            pltpu.VMEM((TILE, 160), BF16),
            pltpu.VMEM((512, TILE), BF16),
            pltpu.VMEM((2, 2, 64, TILE), BF16),
            pltpu.VMEM((2, 2, 64, TILE), BF16),
            pltpu.VMEM((IMG + 32, TILE), BF16),
            pltpu.VMEM((IMG, TILE), F32),
            pltpu.VMEM((3, IMG // 4, TILE), F32),
            pltpu.SemaphoreType.DMA((3,)),
            pltpu.SemaphoreType.DMA((8,)),
            arrivals,
            arrivals,
            arrivals,
            arrivals,
            arrivals,
            pltpu.SemaphoreType.DMA,
            pltpu.SemaphoreType.DMA,
            pltpu.SemaphoreType.DMA,
        ],
        compiler_params=pltpu.CompilerParams(
            collective_id=0, has_side_effects=True, vmem_limit_bytes=54 << 20
        ),
        name="coadd",
    )(picture, variance, planes, sky_columns, basis_rows, basis_cols, coeffs, detect_taps)


def body(
    exposures,
    inv_variance,
    mask_planes,
    sky_columns,
    basis_rows,
    basis_cols,
    match_coeffs,
    detect_taps,
):
    difference, detection = coadd(
        exposures[0, 0],
        inv_variance[0, 0],
        mask_planes[0, 0],
        jnp.transpose(sky_columns, (1, 2, 0)),
        basis_rows,
        basis_cols,
        match_coeffs[0],
        detect_taps,
    )
    return (difference[None, None], detection)


def solution(mesh):
    in_specs = (
        P("sky", "band", None, None),
        P("sky", "band", None, None),
        P("sky", "band", None, None),
        P(),
        P(),
        P(),
        P("sky", "band", None),
        P("band", None),
    )
    out_specs = (P("sky", "band", None, None), P("band", "sky"))
    return jax.shard_map(body, mesh=mesh, in_specs=in_specs, out_specs=out_specs, check_vma=False)
```

```python
import jax
import jax.numpy as jnp
from jax import lax
from jax.experimental import pallas as pl
from jax.experimental.pallas import tpu as pltpu
from jax.sharding import PartitionSpec as P

TILE = 128
NB = 9
TAPS = 25
DTAPS = 31
IMG = 1024
HALO = 12
STRIP = NB * 16
KROWS = 10 * STRIP
CHUNK = 128
STEPS = 512 // CHUNK
HALF = CHUNK // 2
AHEAD = 2
MESH = pl.DeviceIdType.MESH
F32 = jnp.float32
BF16 = jnp.bfloat16


def rows_of(block):
    return pl.ds(pl.multiple_of(block * TILE, TILE), TILE)


def quarter_of(block):
    return pl.ds(pl.multiple_of(block * 256, 256), 256)


def lanes_of(block):
    return pl.ds(pl.multiple_of(block * TILE, TILE), TILE)


def device_of(half, klass, slot):
    if half == 0:
        return 8 * slot + klass
    return 8 * lax.div(klass, 2) + 2 * slot + lax.rem(klass, 2)


def place(half):
    own = lax.axis_index("sky")
    y, rest = lax.div(own, 8), lax.rem(own, 8)
    z, core = lax.div(rest, 2), lax.rem(rest, 2)
    return (2 * y + core, z) if half else (rest, y)


def turned_column(column):
    y, rest = lax.div(column, 8), lax.rem(column, 8)
    return 8 * lax.div(rest, 2) + 2 * y + lax.rem(rest, 2)


def chunk_of(half, step):
    return pl.ds(pl.multiple_of(half * 512 + step * CHUNK, CHUNK), CHUNK)


def half_chunk_of(half, step, low):
    return pl.ds(pl.multiple_of(half * 512 + step * CHUNK + low * HALF, HALF), HALF)


def strip_of(half, step, part):
    return pl.ds(pl.multiple_of(half * 512 + step * CHUNK + part * 32, 32), 32)


def turned(tiles, amount):
    for bit in (1, 2, 4):
        take = jnp.bitwise_and(jnp.full(tiles[0].shape, amount, jnp.int32), bit) != 0
        tiles = [jnp.where(take, tiles[(i + bit) % 8], tiles[i]) for i in range(8)]
    return tiles


def bit_lanes(planes_ref, plane):
    lane = lax.broadcasted_iota(jnp.int32, (8, IMG), 1)
    word = jnp.zeros((8, IMG), jnp.int32)
    first = jnp.zeros((8, IMG), jnp.int32)
    for index in range(35):
        inside = lane >= 30 * index
        word = jnp.where(inside, planes_ref[plane, index], word)
        first = jnp.where(inside, 30 * index, first)
    bit = jnp.bitwise_and(lax.shift_right_logical(word, lane - first), 1)
    return (1 - bit).astype(F32)


def build_taps(cols_ref, rows_ref, coeff_ref, col_mat, row_mat):
    pad = jnp.zeros((1, TILE - TAPS), F32)
    far = jnp.zeros((1, TILE), F32)
    for k in range(NB):
        taps = (cols_ref[k : k + 1, :] * coeff_ref[0, k]).astype(BF16).astype(F32)
        base = pltpu.roll(jnp.concatenate([taps, pad, far], 1), 2 * TILE - HALO, 1)
        ring = pltpu.roll(jnp.broadcast_to(base, (TILE, 2 * TILE)), 0, 1, stride=1, stride_axis=0)
        col_mat[:, k * TILE : (k + 1) * TILE] = ring.T.astype(BF16)
    place_w = lax.broadcasted_iota(jnp.int32, (TILE, 512), 0)
    place_l = lax.broadcasted_iota(jnp.int32, (TILE, 512), 1)
    picker = jnp.where(
        jnp.logical_and(place_l == lax.div(place_w, 16) * STRIP + lax.rem(place_w, 16), place_w < 48),
        1.0,
        0.0,
    ).astype(BF16)
    stacked = []
    for k in range(NB):
        taps = rows_ref[k : k + 1, :].astype(BF16).astype(F32)
        base = pltpu.roll(jnp.concatenate([taps, pad], 1), 4, 1)
        stacked.append(pltpu.roll(jnp.broadcast_to(base, (16, TILE)), 0, 1, stride=1, stride_axis=0))
    spread = jnp.dot(
        jnp.concatenate(stacked, 0).astype(BF16), picker, preferred_element_type=F32
    )
    first = jnp.zeros((16, 512), F32)
    for k in range(NB):
        first = first + pltpu.roll(spread[16 * k : 16 * k + 16], 16 * k, 1)
    first = jnp.concatenate([first, jnp.zeros((16, 1024), F32)], 1)
    for u in range(8):
        row_mat[16 * u : 16 * u + 16, :] = pltpu.roll(first, STRIP * u, 1)[:, :KROWS].astype(BF16)


def column_pass(picture, col_mat, mid):
    mid[0] = jnp.zeros((NB, 16, IMG), BF16)
    mid[65] = jnp.zeros((NB, 16, IMG), BF16)
    near = lax.broadcasted_iota(jnp.int32, (IMG, TILE), 1) < 64

    def one(j, _):
        here = picture[:, lanes_of(j)]
        after = picture[:, lanes_of(jnp.minimum(j + 1, 7))]
        before = picture[:, lanes_of(jnp.maximum(j - 1, 0))]
        zero = jnp.zeros_like(here)
        after = jnp.where(jnp.broadcast_to(j < 7, near.shape), after, zero)
        before = jnp.where(jnp.broadcast_to(j > 0, near.shape), before, zero)
        lhs = jnp.concatenate([here, jnp.where(near, after, before)], 1)
        for k in range(0, NB, 2):
            count = min(2, NB - k)
            got = jnp.dot(
                lhs, col_mat[:, k * TILE : (k + count) * TILE], preferred_element_type=F32
            ).astype(BF16)
            for t in range(count):
                mid[1:65, k + t, :, lanes_of(j)] = got[:, t * TILE : (t + 1) * TILE].reshape(64, 16, TILE)
        return 0

    lax.fori_loop(0, 8, one, 0)


def build_detection(detect_ref, pack_mat, smooth_mat, filter_mat):
    row = lax.broadcasted_iota(jnp.int32, (IMG, 2 * TILE), 0)
    lane = lax.broadcasted_iota(jnp.int32, (IMG, 2 * TILE), 1)
    block, inner = lax.div(row, TILE), lax.rem(row, TILE)
    last = jnp.logical_and(inner >= 112, lane == block * 16 + inner - 112)
    first = jnp.logical_and(inner < 16, lane == TILE + block * 16 + inner)
    pack_mat[...] = jnp.where(jnp.logical_or(last, first), 1.0, 0.0).astype(BF16)
    taps = detect_ref[...].astype(BF16).astype(F32)
    taps = jnp.concatenate(
        [taps, jnp.zeros((1, TILE - DTAPS), F32), jnp.zeros((1, TILE), F32)], 1
    )

    def ring(shift):
        base = jnp.broadcast_to(pltpu.roll(taps, shift, 1), (TILE, 2 * TILE))
        return pltpu.roll(base, 0, 1, stride=1, stride_axis=0)

    table = ring(2 * TILE - 15)
    table = jnp.concatenate([table[:, :TILE].T, table[:, TILE:].T], 0).astype(BF16)
    smooth_mat[0:TILE] = table[0:TILE]
    for b in range(8):
        smooth_mat[TILE + 16 * b : TILE + 16 * b + 16] = table[240:256]
        smooth_mat[2 * TILE + 16 * b : 2 * TILE + 16 * b + 16] = table[128:144]
    filter_mat[...] = ring(1)[:, :160].astype(BF16)


def coadd_kernel(
    picture_in,
    variance_in,
    planes_ref,
    sky_in,
    rows_ref,
    cols_ref,
    coeff_ref,
    detect_ref,
    difference_out,
    detection_out,
    picture,
    variance,
    sky_ref,
    col_keep,
    col_mat,
    row_mat,
    mid,
    matched,
    w_send,
    w_recv,
    m_send,
    m_recv,
    p_send,
    p_recv,
    o_recv,
    numer_own,
    denom_own,
    t_all,
    q_send,
    q_recv,
    flat_ref,
    pack_mat,
    smooth_mat,
    filter_mat,
    natural,
    e_send,
    e_recv,
    smooth,
    power,
    power_out,
    b_recv,
    load_sem,
    send_sem,
    w_sem,
    m_sem,
    p_sem,
    o_sem,
    t_sem,
    f_sem,
    q_sem,
    x_sem,
    e_sem,
    b_sem,
):
    own = lax.axis_index("sky")
    band = lax.axis_index("band")
    barrier = pltpu.get_barrier_semaphore()
    places, group, sources, ring = [], [], [], []
    for half in range(2):
        klass, slot = place(half)
        places.append((klass, slot))
        group.append([device_of(half, lax.rem(klass + d, 8), slot) for d in range(8)])
        sources.append([device_of(half, lax.rem(klass + 8 - d, 8), slot) for d in range(8)])
        ring.append([device_of(half, klass, lax.rem(slot + t, 4)) for t in range(4)])
        for d in range(1, 8):
            pl.semaphore_signal(
                barrier, inc=1, device_id=(group[half][d], band), device_id_type=MESH
            )
    mirror = turned_column(own)
    for step in (1, 31):
        for peer in (
            lax.rem(own + step, 32),
            lax.rem(mirror + step, 32),
            turned_column(lax.rem(own + step, 32)),
        ):
            pl.semaphore_signal(barrier, inc=1, device_id=(peer, band), device_id_type=MESH)
    for step in range(1, 4):
        pl.semaphore_signal(
            barrier, inc=1, device_id=(own, lax.rem(band + step, 4)), device_id_type=MESH
        )

    for z in range(4):
        holder = 8 * places[1][1] + 2 * z + lax.rem(own, 2)

        @pl.when(holder != own)
        def _():
            pl.semaphore_signal(barrier, inc=1, device_id=(holder, band), device_id_type=MESH)

    load_sky = pltpu.make_async_copy(sky_in, sky_ref, load_sem.at[2])
    load_variance = pltpu.make_async_copy(variance_in, variance, load_sem.at[0])
    load_picture = pltpu.make_async_copy(picture_in, picture, load_sem.at[1])
    load_sky.start()
    load_variance.start()
    load_picture.start()
    col_keep[...] = bit_lanes(planes_ref, 0)
    row_keep = bit_lanes(planes_ref, 1)
    for i in range(8):
        flat_ref[i * TILE : (i + 1) * TILE] = jnp.broadcast_to(
            row_keep[0:1, i * TILE : (i + 1) * TILE], (TILE, TILE)
        ).T
    load_sky.wait()
    start = sky_ref[band, 0, own]
    turn = [places[half][0] - start + 32 for half in range(2)]
    load_variance.wait()
    pl.semaphore_wait(barrier, jnp.where(mirror != own, 27, 26))

    def send(src, dst, sem_send, sem_recv, device, to_band=None):
        pltpu.make_async_remote_copy(
            src_ref=src,
            dst_ref=dst,
            send_sem=sem_send,
            recv_sem=sem_recv,
            device_id=(device, band if to_band is None else to_band),
            device_id_type=MESH,
        ).start()

    def wait_for(ref, sem):
        pltpu.make_async_copy(ref, ref, sem).wait()

    def to_group(half, step, src, dst, sem_send, sem_recv):
        rows = chunk_of(half, step)
        for d in range(1, 8):
            send(
                src.at[d, rows], dst.at[d, rows], sem_send, sem_recv.at[half, step], group[half][d]
            )

    def stage_weight(step, _):
        for half in range(2):

            def part(r, _):
                at = strip_of(half, step, r)
                flat = flat_ref[at, :]
                tiles = []
                for c in range(8):
                    keep = flat * col_keep[0:1, c * TILE : (c + 1) * TILE]
                    tiles.append(
                        (variance[at, c * TILE : (c + 1) * TILE].astype(F32) * keep).astype(BF16)
                    )
                for d, tile in enumerate(turned(tiles, turn[half])):
                    w_send[d, at, :] = tile
                return 0

            lax.fori_loop(0, CHUNK // 32, part, 0)
            to_group(half, step, w_send, w_recv, send_sem.at[0], w_sem)
        return 0

    lax.fori_loop(0, STEPS, stage_weight, 0)
    build_taps(cols_ref, rows_ref, coeff_ref, col_mat, row_mat)
    build_detection(detect_ref, pack_mat, smooth_mat, filter_mat)
    load_picture.wait()
    column_pass(picture, col_mat, mid)

    def stage_matched(step, _):
        for half in range(2):

            def block(i, _):
                first = half * 32 + step * (CHUNK // 16) + i * 8
                window = mid[pl.ds(first, 10)].reshape(KROWS, IMG)
                matched[...] = jnp.dot(
                    row_mat[...], window, preferred_element_type=F32
                ).astype(BF16)

                def part(r, _):
                    at = strip_of(half, step, i * 4 + r)
                    inner = pl.ds(pl.multiple_of(r * 32, 32), 32)
                    tiles = [matched[inner, c * TILE : (c + 1) * TILE] for c in range(8)]
                    for d, tile in enumerate(turned(tiles, turn[half])):
                        m_send[d, at, :] = tile
                    return 0

                lax.fori_loop(0, 4, part, 0)
                return 0

            lax.fori_loop(0, CHUNK // TILE, block, 0)
            to_group(half, step, m_send, m_recv, send_sem.at[1], m_sem)
        return 0


    def column_slot(exposure, klass):
        begin = sky_ref[band, 0, exposure]
        c = jnp.bitwise_and(klass - begin + 32, 7)
        return lax.shift_right_logical(jnp.bitwise_and(begin + c, 31), 3)

    def reduce_group(step, _):
        for half in range(2):
            klass, slot = places[half]
            rows = chunk_of(half, step)
            piece = half * STEPS + step
            wait_for(w_recv.at[pl.ds(1, 7), rows], w_sem.at[half, step])
            wait_for(m_recv.at[pl.ds(1, 7), rows], m_sem.at[half, step])
            rel = [
                jnp.full(
                    (32, TILE),
                    jnp.bitwise_and(column_slot(sources[half][d], klass) - slot + 4, 3),
                    jnp.int32,
                )
                for d in range(8)
            ]

            for top in range(2):

                def part(r, _):
                    at = strip_of(half, step, top * (HALF // 32) + r)
                    inner = pl.ds(pl.multiple_of(r * 32, 32), 32)
                    numer = [jnp.zeros((32, TILE), F32) for _ in range(4)]
                    denom = [jnp.zeros((32, TILE), F32) for _ in range(4)]
                    for d in range(8):
                        w = (w_recv if d else w_send)[d, at, :].astype(F32)
                        wm = w * (m_recv if d else m_send)[d, at, :].astype(F32)
                        for t in range(4):
                            hit = rel[d] == t
                            numer[t] = numer[t] + jnp.where(hit, wm, 0.0)
                            denom[t] = denom[t] + jnp.where(hit, w, 0.0)
                    numer_own[at, :] = numer[0]
                    denom_own[at, :] = denom[0]
                    for t in range(1, 4):
                        p_send[t, piece, top, 0, inner, :] = numer[t].astype(BF16)
                        p_send[t, piece, top, 1, inner, :] = denom[t].astype(BF16)
                    return 0

                lax.fori_loop(0, HALF // 32, part, 0)
            after, before = ring[half][1], ring[half][3]
            arrive = p_sem.at[half, step]
            onward = o_sem.at[half, step]
            send(p_send.at[2, piece, 0], o_recv.at[0, piece], send_sem.at[2], onward, after)
            send(p_send.at[2, piece, 1], o_recv.at[1, piece], send_sem.at[2], onward, before)
            send(p_send.at[1, piece, 1], p_recv.at[0, piece, 1], send_sem.at[2], arrive, after)
            send(p_send.at[3, piece, 0], p_recv.at[1, piece, 0], send_sem.at[2], arrive, before)
        return 0

    def combine(step, _):
        for half in range(2):
            piece = half * STEPS + step
            wait_for(o_recv.at[:, piece], o_sem.at[half, step])
            for side, t, top in ((0, 1, 0), (1, 3, 1)):
                for kind in range(2):
                    total = p_send[t, piece, top, kind].astype(F32) + o_recv[
                        side, piece, kind
                    ].astype(F32)
                    p_send[t, piece, top, kind] = total.astype(BF16)
                send(
                    p_send.at[t, piece, top],
                    p_recv.at[side, piece, top],
                    send_sem.at[2],
                    p_sem.at[half, step],
                    ring[half][t],
                )
        return 0

    def make_template(step, _):
        for half in range(2):
            rows = chunk_of(half, step)
            piece = half * STEPS + step
            wait_for(p_recv.at[:, piece], p_sem.at[half, step])
            for top in range(2):

                def part(r, _):
                    at = strip_of(half, step, top * (HALF // 32) + r)
                    inner = pl.ds(pl.multiple_of(r * 32, 32), 32)
                    numer = numer_own[at, :]
                    denom = denom_own[at, :]
                    for side in range(2):
                        numer = numer + p_recv[side, piece, top, 0, inner, :].astype(F32)
                        denom = denom + p_recv[side, piece, top, 1, inner, :].astype(F32)
                    t_all[0, at, :] = (numer / jnp.maximum(denom, 1.0)).astype(BF16)
                    return 0

                lax.fori_loop(0, HALF // 32, part, 0)
            arrive = t_sem.at[half, step]
            send(t_all.at[0, rows], t_all.at[1, rows], send_sem.at[3], arrive, ring[half][1])
            send(t_all.at[0, rows], t_all.at[2, rows], send_sem.at[3], arrive, ring[half][3])
        return 0

    def forward(step, _):
        for half in range(2):
            wait_for(t_all.at[pl.ds(1, 2), chunk_of(half, step)], t_sem.at[half, step])
            arrive = f_sem.at[half, step]
            top, low = half_chunk_of(half, step, 0), half_chunk_of(half, step, 1)
            send(t_all.at[1, top], t_all.at[3, top], send_sem.at[3], arrive, ring[half][1])
            send(t_all.at[2, low], t_all.at[3, low], send_sem.at[3], arrive, ring[half][3])
        return 0

    def send_edges():
        for half in range(2):
            column = mirror if half else own
            wide = jnp.concatenate(
                [t_all[0, half * 512 + 64 * b : half * 512 + 64 * b + 64, :] for b in range(8)], 1
            )
            packed = jnp.dot(wide, pack_mat[...], preferred_element_type=F32).astype(BF16)
            for side in range(2):
                e_send[half, side] = packed[:, side * TILE : (side + 1) * TILE]
                peer = lax.rem(column + (31 if side else 1), 32)
                send(e_send.at[half, side], e_recv.at[half, side], send_sem.at[6], e_sem, peer)

    def send_home(src, into, target, step):
        @pl.when(target != own)
        def _():
            send(src, into, send_sem.at[5], x_sem.at[step], target)

        @pl.when(target == own)
        def _():
            pltpu.make_async_copy(src, into, x_sem.at[step]).start()

    def pick_templates(step, _):
        for half in (1, 0):
            klass, slot = places[half]
            rows = chunk_of(half, step)
            wait_for(t_all.at[3, rows], f_sem.at[half, step])
            if half:
                strip = strip_of(1, step, slot * (CHUNK // TILE))
                into = natural.at[strip_of(0, step, slot * (CHUNK // TILE))]
                for held, t in ((0, 0), (1, 1), (3, 2), (2, 3)):
                    send_home(
                        t_all.at[held, strip], into, 8 * lax.rem(slot + 4 - t, 4) + klass, step
                    )
            rel = [
                jnp.full(
                    (32, TILE),
                    jnp.bitwise_and(slot - column_slot(group[half][d], klass) + 4, 3),
                    jnp.int32,
                )
                for d in range(8)
            ]

            def part(r, _):
                at = strip_of(half, step, r)
                values = [t_all[place, at, :] for place in (0, 1, 3, 2)]
                for d in range(8):
                    value = values[0]
                    for t in range(1, 4):
                        value = jnp.where(rel[d] == t, values[t], value)
                    q_send[d, at, :] = value
                return 0

            lax.fori_loop(0, CHUNK // 32, part, 0)
            to_group(half, step, q_send, q_recv, send_sem.at[4], q_sem)
        return 0

    stages = (
        (stage_matched, -AHEAD),
        (reduce_group, 0),
        (combine, 1),
        (make_template, 2),
        (forward, 3),
        (pick_templates, 4),
    )

    def tick(n, _):
        for stage, lag in stages:
            if lag >= 0:

                @pl.when(jnp.logical_and(n >= lag, n < STEPS + lag))
                def _():
                    stage(n - lag, 0)

            else:

                @pl.when(n < STEPS + lag)
                def _():
                    stage(n - lag, 0)

            if stage is make_template:

                @pl.when(n == STEPS + 1)
                def _():
                    send_edges()

        return 0

    lax.fori_loop(0, AHEAD, stage_matched, 0)
    lax.fori_loop(0, STEPS + 4, tick, 0)
    smooth[0:16] = jnp.zeros((16, TILE), BF16)
    smooth[IMG + 16 : IMG + 32] = jnp.zeros((16, TILE), BF16)
    lane_group = lax.div(lax.broadcasted_iota(jnp.int32, (64, TILE), 1), 16)

    def smooth_rows(i):
        half = i // 4
        pieces = []
        for b in range(2 * (i % 4), 2 * (i % 4) + 2):
            here = (natural if half else t_all.at[0])[64 * b : 64 * b + 64, :]
            zero = jnp.zeros((64, TILE), BF16)
            left = jnp.where(lane_group == b, e_recv[half, 0], zero)
            right = jnp.where(lane_group == b, e_recv[half, 1], zero)
            pieces.append(jnp.concatenate([here, left, right], 1))
        got = jnp.dot(jnp.concatenate(pieces, 0), smooth_mat[...], preferred_element_type=F32)
        smooth[16 + TILE * i : 16 + TILE * i + TILE] = got.astype(BF16)

    def filter_rows(i):
        got = jnp.dot(
            filter_mat[...], smooth[TILE * i : TILE * i + 160], preferred_element_type=F32
        )
        power[TILE * i : TILE * i + TILE] = got * got
        power_out[TILE * i : TILE * i + TILE] = (got * got).astype(BF16)

    def send_power(target):
        @pl.when(target != band)
        def _():
            place_in = lax.rem(band - target + 4, 4) - 1
            send(
                power_out.at[pl.ds(256 * target, 256)],
                b_recv.at[place_in],
                send_sem.at[7],
                b_sem,
                own,
                target,
            )

    wait_for(e_recv, e_sem)
    for i in range(4):
        smooth_rows(i)
    wait_for(natural.at[pl.ds(0, CHUNK)], x_sem.at[0])
    smooth_rows(4)
    for i in range(4):
        filter_rows(i)
    send_power(0)
    send_power(1)
    for step in range(1, STEPS):
        wait_for(natural.at[pl.ds(step * CHUNK, CHUNK)], x_sem.at[step])
    for i in range(5, 8):
        smooth_rows(i)
    for i in range(4, 8):
        filter_rows(i)
    send_power(2)
    send_power(3)

    def subtract(step, _):
        for half in range(2):
            wait_for(q_recv.at[pl.ds(1, 7), chunk_of(half, step)], q_sem.at[half, step])

            def part(r, _):
                at = strip_of(half, step, r)
                tiles = []
                for i in range(8):
                    d = (8 - i) % 8
                    m = m_send[i, at, :].astype(F32)
                    q = (q_recv if d else q_send)[d, at, :].astype(F32)
                    tiles.append((m - q).astype(BF16))
                for c, tile in enumerate(turned(tiles, 64 - turn[half])):
                    difference_out[at, c * TILE : (c + 1) * TILE] = tile
                return 0

            lax.fori_loop(0, CHUNK // 32, part, 0)
        return 0

    lax.fori_loop(0, STEPS, subtract, 0)
    wait_for(b_recv, b_sem)
    detection_out[...] = (
        power[quarter_of(band), :]
        + b_recv[0].astype(F32)
        + b_recv[1].astype(F32)
        + b_recv[2].astype(F32)
    )
    wait_for(w_send.at[pl.ds(1, 7)], send_sem.at[0])
    wait_for(m_send.at[pl.ds(1, 7)], send_sem.at[1])
    wait_for(p_send.at[pl.ds(1, 3)], send_sem.at[2])
    wait_for(t_all.at[pl.ds(1, 3)], send_sem.at[3])
    wait_for(q_send.at[pl.ds(1, 7)], send_sem.at[4])

    @pl.when(mirror != own)
    def _():
        wait_for(natural, send_sem.at[5])

    @pl.when(mirror == own)
    def _():
        wait_for(natural.at[pl.ds(0, 3 * TILE)], send_sem.at[5])

    wait_for(e_send, send_sem.at[6])
    wait_for(b_recv, send_sem.at[7])


def coadd(picture, variance, planes, sky_columns, basis_rows, basis_cols, coeffs, detect_taps):
    vmem = pl.BlockSpec(memory_space=pltpu.VMEM)
    smem = pl.BlockSpec(memory_space=pltpu.SMEM)
    anyw = pl.BlockSpec(memory_space=pl.ANY)
    tiles = pltpu.VMEM((8, IMG, TILE), BF16)
    arrivals = pltpu.SemaphoreType.DMA((2, STEPS))
    return pl.pallas_call(
        coadd_kernel,
        out_shape=(pltpu.VMEM((IMG, IMG), BF16), pltpu.VMEM((IMG // 4, TILE), F32)),
        in_specs=[anyw, anyw, smem, anyw, vmem, vmem, smem, vmem],
        out_specs=(vmem, vmem),
        scratch_shapes=[
            pltpu.VMEM((IMG, IMG), BF16),
            pltpu.VMEM((IMG, IMG), BF16),
            pltpu.SMEM((4, 8, 32), jnp.int32),
            pltpu.VMEM((8, IMG), F32),
            pltpu.VMEM((2 * TILE, NB * TILE), BF16),
            pltpu.VMEM((TILE, KROWS), BF16),
            pltpu.VMEM((66, NB, 16, IMG), BF16),
            pltpu.VMEM((TILE, IMG), BF16),
            tiles,
            tiles,
            tiles,
            tiles,
            pltpu.VMEM((4, 2 * STEPS, 2, 2, HALF, TILE), BF16),
            pltpu.VMEM((2, 2 * STEPS, 2, 2, HALF, TILE), BF16),
            pltpu.VMEM((2, 2 * STEPS, 2, HALF, TILE), BF16),
            pltpu.VMEM((IMG, TILE), F32),
            pltpu.VMEM((IMG, TILE), F32),
            pltpu.VMEM((4, IMG, TILE), BF16),
            tiles,
            tiles,
            pltpu.VMEM((IMG, TILE), F32),
            pltpu.VMEM((IMG, 2 * TILE), BF16),
            pltpu.VMEM((3 * TILE, TILE), BF16),
            pltpu.VMEM((TILE, 160), BF16),
            pltpu.VMEM((512, TILE), BF16),
            pltpu.VMEM((2, 2, 64, TILE), BF16),
            pltpu.VMEM((2, 2, 64, TILE), BF16),
            pltpu.VMEM((IMG + 32, TILE), BF16),
            pltpu.VMEM((IMG, TILE), F32),
            pltpu.VMEM((IMG, TILE), BF16),
            pltpu.VMEM((3, IMG // 4, TILE), BF16),
            pltpu.SemaphoreType.DMA((3,)),
            pltpu.SemaphoreType.DMA((8,)),
            arrivals,
            arrivals,
            arrivals,
            arrivals,
            arrivals,
            arrivals,
            arrivals,
            pltpu.SemaphoreType.DMA((STEPS,)),
            pltpu.SemaphoreType.DMA,
            pltpu.SemaphoreType.DMA,
        ],
        compiler_params=pltpu.CompilerParams(
            collective_id=0, has_side_effects=True, vmem_limit_bytes=54 << 20
        ),
        name="coadd",
    )(picture, variance, planes, sky_columns, basis_rows, basis_cols, coeffs, detect_taps)


def body(
    exposures,
    inv_variance,
    mask_planes,
    sky_columns,
    basis_rows,
    basis_cols,
    match_coeffs,
    detect_taps,
):
    difference, detection = coadd(
        exposures[0, 0],
        inv_variance[0, 0],
        mask_planes[0, 0],
        jnp.transpose(sky_columns, (1, 2, 0)),
        basis_rows,
        basis_cols,
        match_coeffs[0],
        detect_taps,
    )
    return (difference[None, None], detection)


def solution(mesh):
    in_specs = (
        P("sky", "band", None, None),
        P("sky", "band", None, None),
        P("sky", "band", None, None),
        P(),
        P(),
        P(),
        P("sky", "band", None),
        P("band", None),
    )
    out_specs = (P("sky", "band", None, None), P("band", "sky"))
    return jax.shard_map(body, mesh=mesh, in_specs=in_specs, out_specs=out_specs, check_vma=False)
```

```python
import jax
import jax.numpy as jnp
from jax import lax
from jax.experimental import pallas as pl
from jax.experimental.pallas import tpu as pltpu
from jax.sharding import PartitionSpec as P

TILE = 128
NB = 9
TAPS = 25
DTAPS = 31
IMG = 1024
HALO = 12
STRIP = NB * 16
KROWS = 10 * STRIP
CHUNK = 128
STEPS = 512 // CHUNK
HALF = CHUNK // 2
AHEAD = 2
MESH = pl.DeviceIdType.MESH
F32 = jnp.float32
BF16 = jnp.bfloat16


def rows_of(block):
    return pl.ds(pl.multiple_of(block * TILE, TILE), TILE)


def quarter_of(block):
    return pl.ds(pl.multiple_of(block * 256, 256), 256)


def lanes_of(block):
    return pl.ds(pl.multiple_of(block * TILE, TILE), TILE)


def device_of(half, klass, slot):
    if half == 0:
        return 8 * slot + klass
    return 8 * lax.div(klass, 2) + 2 * slot + lax.rem(klass, 2)


def place(half):
    own = lax.axis_index("sky")
    y, rest = lax.div(own, 8), lax.rem(own, 8)
    z, core = lax.div(rest, 2), lax.rem(rest, 2)
    return (2 * y + core, z) if half else (rest, y)


def turned_column(column):
    y, rest = lax.div(column, 8), lax.rem(column, 8)
    return 8 * lax.div(rest, 2) + 2 * y + lax.rem(rest, 2)


def chunk_of(half, step):
    return pl.ds(pl.multiple_of(half * 512 + step * CHUNK, CHUNK), CHUNK)


def half_chunk_of(half, step, low):
    return pl.ds(pl.multiple_of(half * 512 + step * CHUNK + low * HALF, HALF), HALF)


def strip_of(half, step, part):
    return pl.ds(pl.multiple_of(half * 512 + step * CHUNK + part * 32, 32), 32)


def turned(tiles, amount):
    for bit in (1, 2, 4):
        take = jnp.bitwise_and(jnp.full(tiles[0].shape, amount, jnp.int32), bit) != 0
        tiles = [jnp.where(take, tiles[(i + bit) % 8], tiles[i]) for i in range(8)]
    return tiles


def bit_lanes(planes_ref, plane):
    lane = lax.broadcasted_iota(jnp.int32, (8, IMG), 1)
    word = jnp.zeros((8, IMG), jnp.int32)
    first = jnp.zeros((8, IMG), jnp.int32)
    for index in range(35):
        inside = lane >= 30 * index
        word = jnp.where(inside, planes_ref[plane, index], word)
        first = jnp.where(inside, 30 * index, first)
    bit = jnp.bitwise_and(lax.shift_right_logical(word, lane - first), 1)
    return (1 - bit).astype(F32)


def build_taps(cols_ref, rows_ref, coeff_ref, col_mat, row_mat):
    pad = jnp.zeros((1, TILE - TAPS), F32)
    far = jnp.zeros((1, TILE), F32)
    for k in range(NB):
        taps = (cols_ref[k : k + 1, :] * coeff_ref[0, k]).astype(BF16).astype(F32)
        base = pltpu.roll(jnp.concatenate([taps, pad, far], 1), 2 * TILE - HALO, 1)
        ring = pltpu.roll(jnp.broadcast_to(base, (TILE, 2 * TILE)), 0, 1, stride=1, stride_axis=0)
        col_mat[:, k * TILE : (k + 1) * TILE] = ring.T.astype(BF16)
    place_w = lax.broadcasted_iota(jnp.int32, (TILE, 512), 0)
    place_l = lax.broadcasted_iota(jnp.int32, (TILE, 512), 1)
    picker = jnp.where(
        jnp.logical_and(place_l == lax.div(place_w, 16) * STRIP + lax.rem(place_w, 16), place_w < 48),
        1.0,
        0.0,
    ).astype(BF16)
    stacked = []
    for k in range(NB):
        taps = rows_ref[k : k + 1, :].astype(BF16).astype(F32)
        base = pltpu.roll(jnp.concatenate([taps, pad], 1), 4, 1)
        stacked.append(pltpu.roll(jnp.broadcast_to(base, (16, TILE)), 0, 1, stride=1, stride_axis=0))
    spread = jnp.dot(
        jnp.concatenate(stacked, 0).astype(BF16), picker, preferred_element_type=F32
    )
    first = jnp.zeros((16, 512), F32)
    for k in range(NB):
        first = first + pltpu.roll(spread[16 * k : 16 * k + 16], 16 * k, 1)
    first = jnp.concatenate([first, jnp.zeros((16, 1024), F32)], 1)
    for u in range(8):
        row_mat[16 * u : 16 * u + 16, :] = pltpu.roll(first, STRIP * u, 1)[:, :KROWS].astype(BF16)


def column_pass(picture, col_mat, mid):
    mid[0] = jnp.zeros((NB, 16, IMG), BF16)
    mid[65] = jnp.zeros((NB, 16, IMG), BF16)
    near = lax.broadcasted_iota(jnp.int32, (IMG, TILE), 1) < 64

    def one(j, _):
        here = picture[:, lanes_of(j)]
        after = picture[:, lanes_of(jnp.minimum(j + 1, 7))]
        before = picture[:, lanes_of(jnp.maximum(j - 1, 0))]
        zero = jnp.zeros_like(here)
        after = jnp.where(jnp.broadcast_to(j < 7, near.shape), after, zero)
        before = jnp.where(jnp.broadcast_to(j > 0, near.shape), before, zero)
        lhs = jnp.concatenate([here, jnp.where(near, after, before)], 1)
        for k in range(0, NB, 2):
            count = min(2, NB - k)
            got = jnp.dot(
                lhs, col_mat[:, k * TILE : (k + count) * TILE], preferred_element_type=F32
            ).astype(BF16)
            for t in range(count):
                mid[1:65, k + t, :, lanes_of(j)] = got[:, t * TILE : (t + 1) * TILE].reshape(64, 16, TILE)
        return 0

    lax.fori_loop(0, 8, one, 0)


def build_detection(detect_ref, pack_mat, smooth_mat, filter_mat):
    row = lax.broadcasted_iota(jnp.int32, (IMG, 2 * TILE), 0)
    lane = lax.broadcasted_iota(jnp.int32, (IMG, 2 * TILE), 1)
    block, inner = lax.div(row, TILE), lax.rem(row, TILE)
    last = jnp.logical_and(inner >= 112, lane == block * 16 + inner - 112)
    first = jnp.logical_and(inner < 16, lane == TILE + block * 16 + inner)
    pack_mat[...] = jnp.where(jnp.logical_or(last, first), 1.0, 0.0).astype(BF16)
    taps = detect_ref[...].astype(BF16).astype(F32)
    taps = jnp.concatenate(
        [taps, jnp.zeros((1, TILE - DTAPS), F32), jnp.zeros((1, TILE), F32)], 1
    )

    def ring(shift):
        base = jnp.broadcast_to(pltpu.roll(taps, shift, 1), (TILE, 2 * TILE))
        return pltpu.roll(base, 0, 1, stride=1, stride_axis=0)

    table = ring(2 * TILE - 15)
    table = jnp.concatenate([table[:, :TILE].T, table[:, TILE:].T], 0).astype(BF16)
    smooth_mat[0:TILE] = table[0:TILE]
    for b in range(8):
        smooth_mat[TILE + 16 * b : TILE + 16 * b + 16] = table[240:256]
        smooth_mat[2 * TILE + 16 * b : 2 * TILE + 16 * b + 16] = table[128:144]
    filter_mat[...] = ring(1)[:, :160].astype(BF16)


def coadd_kernel(
    picture_in,
    variance_in,
    planes_ref,
    sky_in,
    rows_ref,
    cols_ref,
    coeff_ref,
    detect_ref,
    difference_out,
    detection_out,
    picture,
    variance,
    sky_ref,
    col_keep,
    col_mat,
    row_mat,
    mid,
    matched,
    w_send,
    w_recv,
    m_send,
    m_recv,
    p_send,
    p_recv,
    o_recv,
    numer_own,
    denom_own,
    t_all,
    q_send,
    q_recv,
    flat_ref,
    pack_mat,
    smooth_mat,
    filter_mat,
    natural,
    e_send,
    e_recv,
    smooth,
    power,
    power_out,
    b_recv,
    load_sem,
    send_sem,
    w_sem,
    m_sem,
    p_sem,
    o_sem,
    t_sem,
    f_sem,
    q_sem,
    x_sem,
    e_sem,
    b_sem,
):
    own = lax.axis_index("sky")
    band = lax.axis_index("band")
    barrier = pltpu.get_barrier_semaphore()
    places, group, sources, ring = [], [], [], []
    for half in range(2):
        klass, slot = place(half)
        places.append((klass, slot))
        group.append([device_of(half, lax.rem(klass + d, 8), slot) for d in range(8)])
        sources.append([device_of(half, lax.rem(klass + 8 - d, 8), slot) for d in range(8)])
        ring.append([device_of(half, klass, lax.rem(slot + t, 4)) for t in range(4)])
        for d in range(1, 8):
            pl.semaphore_signal(
                barrier, inc=1, device_id=(group[half][d], band), device_id_type=MESH
            )
    mirror = turned_column(own)
    for step in range(1, 4):
        pl.semaphore_signal(
            barrier, inc=1, device_id=(own, lax.rem(band + step, 4)), device_id_type=MESH
        )

    load_sky = pltpu.make_async_copy(sky_in, sky_ref, load_sem.at[2])
    load_variance = pltpu.make_async_copy(variance_in, variance, load_sem.at[0])
    load_picture = pltpu.make_async_copy(picture_in, picture, load_sem.at[1])
    load_sky.start()
    load_variance.start()
    load_picture.start()
    col_keep[...] = bit_lanes(planes_ref, 0)
    row_keep = bit_lanes(planes_ref, 1)
    for i in range(8):
        flat_ref[i * TILE : (i + 1) * TILE] = jnp.broadcast_to(
            row_keep[0:1, i * TILE : (i + 1) * TILE], (TILE, TILE)
        ).T
    load_sky.wait()
    start = sky_ref[band, 0, own]
    turn = [places[half][0] - start + 32 for half in range(2)]
    load_variance.wait()

    def send(src, dst, sem_send, sem_recv, device, to_band=None):
        pltpu.make_async_remote_copy(
            src_ref=src,
            dst_ref=dst,
            send_sem=sem_send,
            recv_sem=sem_recv,
            device_id=(device, band if to_band is None else to_band),
            device_id_type=MESH,
        ).start()

    def wait_for(ref, sem):
        pltpu.make_async_copy(ref, ref, sem).wait()

    def to_group(half, step, src, dst, sem_send, sem_recv):
        rows = chunk_of(half, step)
        for d in range(1, 8):
            send(
                src.at[d, rows], dst.at[d, rows], sem_send, sem_recv.at[half, step], group[half][d]
            )

    def stage_weight(step, _):
        for half in range(2):

            def part(r, _):
                at = strip_of(half, step, r)
                flat = flat_ref[at, :]
                tiles = []
                for c in range(8):
                    keep = flat * col_keep[0:1, c * TILE : (c + 1) * TILE]
                    tiles.append(
                        (variance[at, c * TILE : (c + 1) * TILE].astype(F32) * keep).astype(BF16)
                    )
                for d, tile in enumerate(turned(tiles, turn[half])):
                    w_send[d, at, :] = tile
                return 0

            lax.fori_loop(0, CHUNK // 32, part, 0)
        return 0

    lax.fori_loop(0, STEPS, stage_weight, 0)
    pl.semaphore_wait(barrier, 17)
    for half in range(2):
        rows = pl.ds(512 * half, 512)
        for d in range(1, 8):
            send(
                w_send.at[d, rows],
                w_recv.at[d, rows],
                send_sem.at[0],
                w_sem.at[half],
                group[half][d],
            )
    build_taps(cols_ref, rows_ref, coeff_ref, col_mat, row_mat)
    build_detection(detect_ref, pack_mat, smooth_mat, filter_mat)
    load_picture.wait()
    column_pass(picture, col_mat, mid)

    def stage_matched(step, _):
        for half in range(2):

            def block(i, _):
                first = half * 32 + step * (CHUNK // 16) + i * 8
                window = mid[pl.ds(first, 10)].reshape(KROWS, IMG)
                matched[...] = jnp.dot(
                    row_mat[...], window, preferred_element_type=F32
                ).astype(BF16)

                def part(r, _):
                    at = strip_of(half, step, i * 4 + r)
                    inner = pl.ds(pl.multiple_of(r * 32, 32), 32)
                    tiles = [matched[inner, c * TILE : (c + 1) * TILE] for c in range(8)]
                    for d, tile in enumerate(turned(tiles, turn[half])):
                        m_send[d, at, :] = tile
                    return 0

                lax.fori_loop(0, 4, part, 0)
                return 0

            lax.fori_loop(0, CHUNK // TILE, block, 0)
            to_group(half, step, m_send, m_recv, send_sem.at[1], m_sem)
        return 0


    def column_slot(exposure, klass):
        begin = sky_ref[band, 0, exposure]
        c = jnp.bitwise_and(klass - begin + 32, 7)
        return lax.shift_right_logical(jnp.bitwise_and(begin + c, 31), 3)

    def reduce_group(step, _):
        for half in (1, 0):
            klass, slot = places[half]
            rows = chunk_of(half, step)
            piece = half * STEPS + step

            @pl.when(step == 0)
            def _():
                wait_for(w_recv.at[pl.ds(1, 7), pl.ds(512 * half, 512)], w_sem.at[half])

            wait_for(m_recv.at[pl.ds(1, 7), rows], m_sem.at[half, step])
            rel = [
                jnp.full(
                    (32, TILE),
                    jnp.bitwise_and(column_slot(sources[half][d], klass) - slot + 4, 3),
                    jnp.int32,
                )
                for d in range(8)
            ]

            for top in range(2):

                def part(r, _):
                    at = strip_of(half, step, top * (HALF // 32) + r)
                    inner = pl.ds(pl.multiple_of(r * 32, 32), 32)
                    numer = [jnp.zeros((32, TILE), F32) for _ in range(4)]
                    denom = [jnp.zeros((32, TILE), F32) for _ in range(4)]
                    for d in range(8):
                        w = (w_recv if d else w_send)[d, at, :].astype(F32)
                        wm = w * (m_recv if d else m_send)[d, at, :].astype(F32)
                        for t in range(4):
                            hit = rel[d] == t
                            numer[t] = numer[t] + jnp.where(hit, wm, 0.0)
                            denom[t] = denom[t] + jnp.where(hit, w, 0.0)
                    numer_own[at, :] = numer[0]
                    denom_own[at, :] = denom[0]
                    for t in range(1, 4):
                        p_send[t, piece, top, 0, inner, :] = numer[t].astype(BF16)
                        p_send[t, piece, top, 1, inner, :] = denom[t].astype(BF16)
                    return 0

                lax.fori_loop(0, HALF // 32, part, 0)
            after, before = ring[half][1], ring[half][3]
            arrive = p_sem.at[half, step]
            onward = o_sem.at[half, step]
            send(p_send.at[2, piece, 0], o_recv.at[0, piece], send_sem.at[2], onward, after)
            send(p_send.at[2, piece, 1], o_recv.at[1, piece], send_sem.at[2], onward, before)
            send(p_send.at[1, piece, 1], p_recv.at[0, piece, 1], send_sem.at[2], arrive, after)
            send(p_send.at[3, piece, 0], p_recv.at[1, piece, 0], send_sem.at[2], arrive, before)
        return 0

    def combine(step, _):
        for half in (1, 0):
            piece = half * STEPS + step
            wait_for(o_recv.at[:, piece], o_sem.at[half, step])
            for side, t, top in ((0, 1, 0), (1, 3, 1)):
                for kind in range(2):
                    total = p_send[t, piece, top, kind].astype(F32) + o_recv[
                        side, piece, kind
                    ].astype(F32)
                    p_send[t, piece, top, kind] = total.astype(BF16)
                send(
                    p_send.at[t, piece, top],
                    p_recv.at[side, piece, top],
                    send_sem.at[2],
                    p_sem.at[half, step],
                    ring[half][t],
                )
        return 0

    def make_template(step, _):
        for half in (1, 0):
            rows = chunk_of(half, step)
            piece = half * STEPS + step
            wait_for(p_recv.at[:, piece], p_sem.at[half, step])
            for top in range(2):

                def part(r, _):
                    at = strip_of(half, step, top * (HALF // 32) + r)
                    inner = pl.ds(pl.multiple_of(r * 32, 32), 32)
                    numer = numer_own[at, :]
                    denom = denom_own[at, :]
                    for side in range(2):
                        numer = numer + p_recv[side, piece, top, 0, inner, :].astype(F32)
                        denom = denom + p_recv[side, piece, top, 1, inner, :].astype(F32)
                    t_all[0, at, :] = (numer / jnp.maximum(denom, 1.0)).astype(BF16)
                    return 0

                lax.fori_loop(0, HALF // 32, part, 0)
            arrive = t_sem.at[half, step]
            send(t_all.at[0, rows], t_all.at[1, rows], send_sem.at[3], arrive, ring[half][1])
            send(t_all.at[0, rows], t_all.at[2, rows], send_sem.at[3], arrive, ring[half][3])
        return 0

    def forward(step, _):
        for half in (1, 0):
            wait_for(t_all.at[pl.ds(1, 2), chunk_of(half, step)], t_sem.at[half, step])
            arrive = f_sem.at[half, step]
            top, low = half_chunk_of(half, step, 0), half_chunk_of(half, step, 1)
            send(t_all.at[1, top], t_all.at[3, top], send_sem.at[3], arrive, ring[half][1])
            send(t_all.at[2, low], t_all.at[3, low], send_sem.at[3], arrive, ring[half][3])
        return 0

    def send_edges():
        for half in range(2):
            column = mirror if half else own
            wide = jnp.concatenate(
                [t_all[0, half * 512 + 64 * b : half * 512 + 64 * b + 64, :] for b in range(8)], 1
            )
            packed = jnp.dot(wide, pack_mat[...], preferred_element_type=F32).astype(BF16)
            for side in range(2):
                e_send[half, side] = packed[:, side * TILE : (side + 1) * TILE]
                peer = lax.rem(column + (31 if side else 1), 32)
                send(e_send.at[half, side], e_recv.at[half, side], send_sem.at[6], e_sem, peer)

    def send_home(src, into, target, step):
        @pl.when(target != own)
        def _():
            send(src, into, send_sem.at[5], x_sem.at[step], target)

        @pl.when(target == own)
        def _():
            pltpu.make_async_copy(src, into, x_sem.at[step]).start()

    def pick_templates(step, _):
        for half in (1, 0):
            klass, slot = places[half]
            rows = chunk_of(half, step)
            wait_for(t_all.at[3, rows], f_sem.at[half, step])
            if half:
                strip = strip_of(1, step, slot * (CHUNK // TILE))
                into = natural.at[strip_of(0, step, slot * (CHUNK // TILE))]
                for held, t in ((0, 0), (1, 1), (3, 2), (2, 3)):
                    send_home(
                        t_all.at[held, strip], into, 8 * lax.rem(slot + 4 - t, 4) + klass, step
                    )
            rel = [
                jnp.full(
                    (32, TILE),
                    jnp.bitwise_and(slot - column_slot(group[half][d], klass) + 4, 3),
                    jnp.int32,
                )
                for d in range(8)
            ]

            def part(r, _):
                at = strip_of(half, step, r)
                values = [t_all[place, at, :] for place in (0, 1, 3, 2)]
                for d in range(8):
                    value = values[0]
                    for t in range(1, 4):
                        value = jnp.where(rel[d] == t, values[t], value)
                    q_send[d, at, :] = value
                return 0

            lax.fori_loop(0, CHUNK // 32, part, 0)
            to_group(half, step, q_send, q_recv, send_sem.at[4], q_sem)
        return 0

    def subtract(step, _):
        for half in range(2):
            wait_for(q_recv.at[pl.ds(1, 7), chunk_of(half, step)], q_sem.at[half, step])

            def part(r, _):
                at = strip_of(half, step, r)
                tiles = []
                for i in range(8):
                    d = (8 - i) % 8
                    m = m_send[i, at, :].astype(F32)
                    q = (q_recv if d else q_send)[d, at, :].astype(F32)
                    tiles.append((m - q).astype(BF16))
                for c, tile in enumerate(turned(tiles, 64 - turn[half])):
                    difference_out[at, c * TILE : (c + 1) * TILE] = tile
                return 0

            lax.fori_loop(0, CHUNK // 32, part, 0)
        return 0

    smooth[0:16] = jnp.zeros((16, TILE), BF16)
    smooth[IMG + 16 : IMG + 32] = jnp.zeros((16, TILE), BF16)
    lane_group = lax.div(lax.broadcasted_iota(jnp.int32, (64, TILE), 1), 16)

    def smooth_rows(i):
        half = i // 4
        pieces = []
        for b in range(2 * (i % 4), 2 * (i % 4) + 2):
            here = (natural if half else t_all.at[0])[64 * b : 64 * b + 64, :]
            zero = jnp.zeros((64, TILE), BF16)
            left = jnp.where(lane_group == b, e_recv[half, 0], zero)
            right = jnp.where(lane_group == b, e_recv[half, 1], zero)
            pieces.append(jnp.concatenate([here, left, right], 1))
        got = jnp.dot(jnp.concatenate(pieces, 0), smooth_mat[...], preferred_element_type=F32)
        smooth[16 + TILE * i : 16 + TILE * i + TILE] = got.astype(BF16)

    def filter_rows(i):
        got = jnp.dot(
            filter_mat[...], smooth[TILE * i : TILE * i + 160], preferred_element_type=F32
        )
        power[TILE * i : TILE * i + TILE] = got * got
        power_out[TILE * i : TILE * i + TILE] = (got * got).astype(BF16)

    def send_power(target):
        @pl.when(target != band)
        def _():
            place_in = lax.rem(band - target + 4, 4) - 1
            send(
                power_out.at[pl.ds(256 * target, 256)],
                b_recv.at[place_in],
                send_sem.at[7],
                b_sem,
                own,
                target,
            )

    def upper_detection():
        wait_for(e_recv, e_sem)
        for i in range(4):
            smooth_rows(i)
        wait_for(natural.at[pl.ds(0, CHUNK)], x_sem.at[0])
        smooth_rows(4)
        for i in range(4):
            filter_rows(i)
        send_power(0)
        send_power(1)

    stages = (
        (stage_matched, -AHEAD),
        (reduce_group, 0),
        (combine, 1),
        (make_template, 2),
        (forward, 3),
        (pick_templates, 4),
    )

    def tick(n, _):
        @pl.when(n == STEPS + 3)
        def _():
            upper_detection()

        for stage, lag in stages:
            if lag >= 0:

                @pl.when(jnp.logical_and(n >= lag, n < STEPS + lag))
                def _():
                    stage(n - lag, 0)

            else:

                @pl.when(n < STEPS + lag)
                def _():
                    stage(n - lag, 0)

            if stage is make_template:

                @pl.when(n == STEPS + 1)
                def _():
                    send_edges()

        return 0

    lax.fori_loop(0, AHEAD, stage_matched, 0)
    lax.fori_loop(0, STEPS + 4, tick, 0)
    lax.fori_loop(0, 1, subtract, 0)
    for step in range(1, STEPS):
        wait_for(natural.at[pl.ds(step * CHUNK, CHUNK)], x_sem.at[step])
    for i in range(5, 8):
        smooth_rows(i)
    for i in range(4, 8):
        filter_rows(i)
    send_power(2)
    send_power(3)

    lax.fori_loop(1, STEPS, subtract, 0)
    wait_for(b_recv, b_sem)
    detection_out[...] = (
        power[quarter_of(band), :]
        + b_recv[0].astype(F32)
        + b_recv[1].astype(F32)
        + b_recv[2].astype(F32)
    )
    wait_for(w_send.at[pl.ds(1, 7)], send_sem.at[0])
    wait_for(m_send.at[pl.ds(1, 7)], send_sem.at[1])
    wait_for(p_send.at[pl.ds(1, 3)], send_sem.at[2])
    wait_for(t_all.at[pl.ds(1, 3)], send_sem.at[3])
    wait_for(q_send.at[pl.ds(1, 7)], send_sem.at[4])

    @pl.when(mirror != own)
    def _():
        wait_for(natural, send_sem.at[5])

    @pl.when(mirror == own)
    def _():
        wait_for(natural.at[pl.ds(0, 3 * TILE)], send_sem.at[5])

    wait_for(e_send, send_sem.at[6])
    wait_for(b_recv, send_sem.at[7])


def coadd(picture, variance, planes, sky_columns, basis_rows, basis_cols, coeffs, detect_taps):
    vmem = pl.BlockSpec(memory_space=pltpu.VMEM)
    smem = pl.BlockSpec(memory_space=pltpu.SMEM)
    anyw = pl.BlockSpec(memory_space=pl.ANY)
    tiles = pltpu.VMEM((8, IMG, TILE), BF16)
    arrivals = pltpu.SemaphoreType.DMA((2, STEPS))
    return pl.pallas_call(
        coadd_kernel,
        out_shape=(pltpu.VMEM((IMG, IMG), BF16), pltpu.VMEM((IMG // 4, TILE), F32)),
        in_specs=[anyw, anyw, smem, anyw, vmem, vmem, smem, vmem],
        out_specs=(vmem, vmem),
        scratch_shapes=[
            pltpu.VMEM((IMG, IMG), BF16),
            pltpu.VMEM((IMG, IMG), BF16),
            pltpu.SMEM((4, 8, 32), jnp.int32),
            pltpu.VMEM((8, IMG), F32),
            pltpu.VMEM((2 * TILE, NB * TILE), BF16),
            pltpu.VMEM((TILE, KROWS), BF16),
            pltpu.VMEM((66, NB, 16, IMG), BF16),
            pltpu.VMEM((TILE, IMG), BF16),
            tiles,
            tiles,
            tiles,
            tiles,
            pltpu.VMEM((4, 2 * STEPS, 2, 2, HALF, TILE), BF16),
            pltpu.VMEM((2, 2 * STEPS, 2, 2, HALF, TILE), BF16),
            pltpu.VMEM((2, 2 * STEPS, 2, HALF, TILE), BF16),
            pltpu.VMEM((IMG, TILE), F32),
            pltpu.VMEM((IMG, TILE), F32),
            pltpu.VMEM((4, IMG, TILE), BF16),
            tiles,
            tiles,
            pltpu.VMEM((IMG, TILE), F32),
            pltpu.VMEM((IMG, 2 * TILE), BF16),
            pltpu.VMEM((3 * TILE, TILE), BF16),
            pltpu.VMEM((TILE, 160), BF16),
            pltpu.VMEM((512, TILE), BF16),
            pltpu.VMEM((2, 2, 64, TILE), BF16),
            pltpu.VMEM((2, 2, 64, TILE), BF16),
            pltpu.VMEM((IMG + 32, TILE), BF16),
            pltpu.VMEM((IMG, TILE), F32),
            pltpu.VMEM((IMG, TILE), BF16),
            pltpu.VMEM((3, IMG // 4, TILE), BF16),
            pltpu.SemaphoreType.DMA((3,)),
            pltpu.SemaphoreType.DMA((8,)),
            pltpu.SemaphoreType.DMA((2,)),
            arrivals,
            arrivals,
            arrivals,
            arrivals,
            arrivals,
            arrivals,
            pltpu.SemaphoreType.DMA((STEPS,)),
            pltpu.SemaphoreType.DMA,
            pltpu.SemaphoreType.DMA,
        ],
        compiler_params=pltpu.CompilerParams(
            collective_id=0, has_side_effects=True, vmem_limit_bytes=54 << 20
        ),
        name="coadd",
    )(picture, variance, planes, sky_columns, basis_rows, basis_cols, coeffs, detect_taps)


def body(
    exposures,
    inv_variance,
    mask_planes,
    sky_columns,
    basis_rows,
    basis_cols,
    match_coeffs,
    detect_taps,
):
    difference, detection = coadd(
        exposures[0, 0],
        inv_variance[0, 0],
        mask_planes[0, 0],
        jnp.transpose(sky_columns, (1, 2, 0)),
        basis_rows,
        basis_cols,
        match_coeffs[0],
        detect_taps,
    )
    return (difference[None, None], detection)


def solution(mesh):
    in_specs = (
        P("sky", "band", None, None),
        P("sky", "band", None, None),
        P("sky", "band", None, None),
        P(),
        P(),
        P(),
        P("sky", "band", None),
        P("band", None),
    )
    out_specs = (P("sky", "band", None, None), P("band", "sky"))
    return jax.shard_map(body, mesh=mesh, in_specs=in_specs, out_specs=out_specs, check_vma=False)
```

```python
import jax
import jax.numpy as jnp
from jax import lax
from jax.experimental import pallas as pl
from jax.experimental.pallas import tpu as pltpu
from jax.sharding import PartitionSpec as P

TILE = 128
NB = 9
TAPS = 25
DTAPS = 31
IMG = 1024
HALO = 12
STRIP = NB * 16
KROWS = 10 * STRIP
CHUNK = 128
STEPS = 512 // CHUNK
HALF = CHUNK // 2
AHEAD = 2
MESH = pl.DeviceIdType.MESH
F32 = jnp.float32
BF16 = jnp.bfloat16


def rows_of(block):
    return pl.ds(pl.multiple_of(block * TILE, TILE), TILE)


def quarter_of(block):
    return pl.ds(pl.multiple_of(block * 256, 256), 256)


def lanes_of(block):
    return pl.ds(pl.multiple_of(block * TILE, TILE), TILE)


def device_of(half, klass, slot):
    if half == 0:
        return 8 * slot + klass
    return 8 * lax.div(klass, 2) + 2 * slot + lax.rem(klass, 2)


def place(half):
    own = lax.axis_index("sky")
    y, rest = lax.div(own, 8), lax.rem(own, 8)
    z, core = lax.div(rest, 2), lax.rem(rest, 2)
    return (2 * y + core, z) if half else (rest, y)


def turned_column(column):
    y, rest = lax.div(column, 8), lax.rem(column, 8)
    return 8 * lax.div(rest, 2) + 2 * y + lax.rem(rest, 2)


def chunk_of(half, step):
    return pl.ds(pl.multiple_of(half * 512 + step * CHUNK, CHUNK), CHUNK)


def half_chunk_of(half, step, low):
    return pl.ds(pl.multiple_of(half * 512 + step * CHUNK + low * HALF, HALF), HALF)


def strip_of(half, step, part):
    return pl.ds(pl.multiple_of(half * 512 + step * CHUNK + part * 32, 32), 32)


def turned(tiles, amount):
    for bit in (1, 2, 4):
        take = jnp.bitwise_and(jnp.full(tiles[0].shape, amount, jnp.int32), bit) != 0
        tiles = [jnp.where(take, tiles[(i + bit) % 8], tiles[i]) for i in range(8)]
    return tiles


def bit_lanes(planes_ref, plane):
    lane = lax.broadcasted_iota(jnp.int32, (8, IMG), 1)
    word = jnp.zeros((8, IMG), jnp.int32)
    first = jnp.zeros((8, IMG), jnp.int32)
    for index in range(35):
        inside = lane >= 30 * index
        word = jnp.where(inside, planes_ref[plane, index], word)
        first = jnp.where(inside, 30 * index, first)
    bit = jnp.bitwise_and(lax.shift_right_logical(word, lane - first), 1)
    return (1 - bit).astype(F32)


def build_taps(cols_ref, rows_ref, coeff_ref, col_mat, row_mat):
    pad = jnp.zeros((1, TILE - TAPS), F32)
    far = jnp.zeros((1, TILE), F32)
    for k in range(NB):
        taps = (cols_ref[k : k + 1, :] * coeff_ref[0, k]).astype(BF16).astype(F32)
        base = pltpu.roll(jnp.concatenate([taps, pad, far], 1), 2 * TILE - HALO, 1)
        ring = pltpu.roll(jnp.broadcast_to(base, (TILE, 2 * TILE)), 0, 1, stride=1, stride_axis=0)
        col_mat[:, k * TILE : (k + 1) * TILE] = ring.T.astype(BF16)
    place_w = lax.broadcasted_iota(jnp.int32, (TILE, 512), 0)
    place_l = lax.broadcasted_iota(jnp.int32, (TILE, 512), 1)
    picker = jnp.where(
        jnp.logical_and(place_l == lax.div(place_w, 16) * STRIP + lax.rem(place_w, 16), place_w < 48),
        1.0,
        0.0,
    ).astype(BF16)
    stacked = []
    for k in range(NB):
        taps = rows_ref[k : k + 1, :].astype(BF16).astype(F32)
        base = pltpu.roll(jnp.concatenate([taps, pad], 1), 4, 1)
        stacked.append(pltpu.roll(jnp.broadcast_to(base, (16, TILE)), 0, 1, stride=1, stride_axis=0))
    spread = jnp.dot(
        jnp.concatenate(stacked, 0).astype(BF16), picker, preferred_element_type=F32
    )
    first = jnp.zeros((16, 512), F32)
    for k in range(NB):
        first = first + pltpu.roll(spread[16 * k : 16 * k + 16], 16 * k, 1)
    first = jnp.concatenate([first, jnp.zeros((16, 1024), F32)], 1)
    for u in range(8):
        row_mat[16 * u : 16 * u + 16, :] = pltpu.roll(first, STRIP * u, 1)[:, :KROWS].astype(BF16)


def column_pass(picture, col_mat, mid):
    mid[0] = jnp.zeros((NB, 16, IMG), BF16)
    mid[65] = jnp.zeros((NB, 16, IMG), BF16)
    near = lax.broadcasted_iota(jnp.int32, (IMG, TILE), 1) < 64

    def one(j, _):
        here = picture[:, lanes_of(j)]
        after = picture[:, lanes_of(jnp.minimum(j + 1, 7))]
        before = picture[:, lanes_of(jnp.maximum(j - 1, 0))]
        zero = jnp.zeros_like(here)
        after = jnp.where(jnp.broadcast_to(j < 7, near.shape), after, zero)
        before = jnp.where(jnp.broadcast_to(j > 0, near.shape), before, zero)
        lhs = jnp.concatenate([here, jnp.where(near, after, before)], 1)
        for k in range(0, NB, 2):
            count = min(2, NB - k)
            got = jnp.dot(
                lhs, col_mat[:, k * TILE : (k + count) * TILE], preferred_element_type=F32
            ).astype(BF16)
            for t in range(count):
                mid[1:65, k + t, :, lanes_of(j)] = got[:, t * TILE : (t + 1) * TILE].reshape(64, 16, TILE)
        return 0

    lax.fori_loop(0, 8, one, 0)


def build_detection(detect_ref, pack_mat, smooth_mat, filter_mat):
    row = lax.broadcasted_iota(jnp.int32, (IMG, 2 * TILE), 0)
    lane = lax.broadcasted_iota(jnp.int32, (IMG, 2 * TILE), 1)
    block, inner = lax.div(row, TILE), lax.rem(row, TILE)
    last = jnp.logical_and(inner >= 112, lane == block * 16 + inner - 112)
    first = jnp.logical_and(inner < 16, lane == TILE + block * 16 + inner)
    pack_mat[...] = jnp.where(jnp.logical_or(last, first), 1.0, 0.0).astype(BF16)
    taps = detect_ref[...].astype(BF16).astype(F32)
    taps = jnp.concatenate(
        [taps, jnp.zeros((1, TILE - DTAPS), F32), jnp.zeros((1, TILE), F32)], 1
    )

    def ring(shift):
        base = jnp.broadcast_to(pltpu.roll(taps, shift, 1), (TILE, 2 * TILE))
        return pltpu.roll(base, 0, 1, stride=1, stride_axis=0)

    table = ring(2 * TILE - 15)
    table = jnp.concatenate([table[:, :TILE].T, table[:, TILE:].T], 0).astype(BF16)
    smooth_mat[0:TILE] = table[0:TILE]
    for b in range(8):
        smooth_mat[TILE + 16 * b : TILE + 16 * b + 16] = table[240:256]
        smooth_mat[2 * TILE + 16 * b : 2 * TILE + 16 * b + 16] = table[128:144]
    filter_mat[...] = ring(1)[:, :160].astype(BF16)


def coadd_kernel(
    picture_in,
    variance_in,
    planes_ref,
    sky_in,
    rows_ref,
    cols_ref,
    coeff_ref,
    detect_ref,
    difference_out,
    detection_out,
    picture,
    variance,
    sky_ref,
    col_keep,
    col_mat,
    row_mat,
    mid,
    matched,
    w_send,
    w_recv,
    m_send,
    m_recv,
    p_send,
    p_recv,
    o_recv,
    numer_own,
    denom_own,
    t_all,
    q_send,
    q_recv,
    flat_ref,
    pack_mat,
    smooth_mat,
    filter_mat,
    natural,
    e_send,
    e_recv,
    smooth,
    power,
    power_out,
    b_recv,
    load_sem,
    send_sem,
    w_sem,
    m_sem,
    p_sem,
    o_sem,
    t_sem,
    f_sem,
    q_sem,
    x_sem,
    e_sem,
    b_sem,
):
    own = lax.axis_index("sky")
    band = lax.axis_index("band")
    barrier = pltpu.get_barrier_semaphore()
    places, group, sources, ring = [], [], [], []
    for half in range(2):
        klass, slot = place(half)
        places.append((klass, slot))
        group.append([device_of(half, lax.rem(klass + d, 8), slot) for d in range(8)])
        sources.append([device_of(half, lax.rem(klass + 8 - d, 8), slot) for d in range(8)])
        ring.append([device_of(half, klass, lax.rem(slot + t, 4)) for t in range(4)])
        for d in range(1, 8):
            pl.semaphore_signal(
                barrier, inc=1, device_id=(group[half][d], band), device_id_type=MESH
            )
    mirror = turned_column(own)
    for step in range(1, 4):
        pl.semaphore_signal(
            barrier, inc=1, device_id=(own, lax.rem(band + step, 4)), device_id_type=MESH
        )

    load_sky = pltpu.make_async_copy(sky_in, sky_ref, load_sem.at[2])
    load_variance = pltpu.make_async_copy(variance_in, variance, load_sem.at[0])
    load_picture = pltpu.make_async_copy(picture_in, picture, load_sem.at[1])
    load_sky.start()
    load_variance.start()
    load_picture.start()
    col_keep[...] = bit_lanes(planes_ref, 0)
    row_keep = bit_lanes(planes_ref, 1)
    for i in range(8):
        flat_ref[i * TILE : (i + 1) * TILE] = jnp.broadcast_to(
            row_keep[0:1, i * TILE : (i + 1) * TILE], (TILE, TILE)
        ).T
    load_sky.wait()
    start = sky_ref[band, 0, own]
    turn = [places[half][0] - start + 32 for half in range(2)]
    load_variance.wait()

    def send(src, dst, sem_send, sem_recv, device, to_band=None):
        pltpu.make_async_remote_copy(
            src_ref=src,
            dst_ref=dst,
            send_sem=sem_send,
            recv_sem=sem_recv,
            device_id=(device, band if to_band is None else to_band),
            device_id_type=MESH,
        ).start()

    def wait_for(ref, sem):
        pltpu.make_async_copy(ref, ref, sem).wait()

    def to_group(half, step, src, dst, sem_send, sem_recv):
        rows = chunk_of(half, step)
        for d in range(1, 8):
            send(
                src.at[d, rows], dst.at[d, rows], sem_send, sem_recv.at[half, step], group[half][d]
            )

    def stage_weight(step, _):
        for half in range(2):

            def part(r, _):
                at = strip_of(half, step, r)
                flat = flat_ref[at, :]
                tiles = []
                for c in range(8):
                    keep = flat * col_keep[0:1, c * TILE : (c + 1) * TILE]
                    tiles.append(
                        (variance[at, c * TILE : (c + 1) * TILE].astype(F32) * keep).astype(BF16)
                    )
                for d, tile in enumerate(turned(tiles, turn[half])):
                    w_send[d, at, :] = tile
                return 0

            lax.fori_loop(0, CHUNK // 32, part, 0)
        return 0

    lax.fori_loop(0, STEPS, stage_weight, 0)
    pl.semaphore_wait(barrier, 17)
    for half in range(2):
        rows = pl.ds(512 * half, 512)
        for d in range(1, 8):
            send(
                w_send.at[d, rows],
                w_recv.at[d, rows],
                send_sem.at[0],
                w_sem.at[half],
                group[half][d],
            )
    build_taps(cols_ref, rows_ref, coeff_ref, col_mat, row_mat)
    build_detection(detect_ref, pack_mat, smooth_mat, filter_mat)
    load_picture.wait()
    column_pass(picture, col_mat, mid)

    def stage_matched(step, _):
        for half in range(2):

            def block(i, _):
                first = half * 32 + step * (CHUNK // 16) + i * 8
                window = mid[pl.ds(first, 10)].reshape(KROWS, IMG)
                matched[...] = jnp.dot(
                    row_mat[...], window, preferred_element_type=F32
                ).astype(BF16)

                def part(r, _):
                    at = strip_of(half, step, i * 4 + r)
                    inner = pl.ds(pl.multiple_of(r * 32, 32), 32)
                    tiles = [matched[inner, c * TILE : (c + 1) * TILE] for c in range(8)]
                    for d, tile in enumerate(turned(tiles, turn[half])):
                        m_send[d, at, :] = tile
                    return 0

                lax.fori_loop(0, 4, part, 0)
                return 0

            lax.fori_loop(0, CHUNK // TILE, block, 0)
            to_group(half, step, m_send, m_recv, send_sem.at[1], m_sem)
        return 0


    def column_slot(exposure, klass):
        begin = sky_ref[band, 0, exposure]
        c = jnp.bitwise_and(klass - begin + 32, 7)
        return lax.shift_right_logical(jnp.bitwise_and(begin + c, 31), 3)

    def reduce_group(step, _):
        for half in (1, 0):
            klass, slot = places[half]
            rows = chunk_of(half, step)
            piece = half * STEPS + step

            @pl.when(step == 0)
            def _():
                wait_for(w_recv.at[pl.ds(1, 7), pl.ds(512 * half, 512)], w_sem.at[half])

            wait_for(m_recv.at[pl.ds(1, 7), rows], m_sem.at[half, step])
            rel = [
                jnp.full(
                    (32, TILE),
                    jnp.bitwise_and(column_slot(sources[half][d], klass) - slot + 4, 3),
                    jnp.int32,
                )
                for d in range(8)
            ]

            for top in range(2):

                def part(r, _):
                    at = strip_of(half, step, top * (HALF // 32) + r)
                    inner = pl.ds(pl.multiple_of(r * 32, 32), 32)
                    numer = [jnp.zeros((32, TILE), F32) for _ in range(4)]
                    denom = [jnp.zeros((32, TILE), F32) for _ in range(4)]
                    for d in range(8):
                        w = (w_recv if d else w_send)[d, at, :].astype(F32)
                        wm = w * (m_recv if d else m_send)[d, at, :].astype(F32)
                        for t in range(4):
                            hit = rel[d] == t
                            numer[t] = numer[t] + jnp.where(hit, wm, 0.0)
                            denom[t] = denom[t] + jnp.where(hit, w, 0.0)
                    numer_own[at, :] = numer[0]
                    denom_own[at, :] = denom[0]
                    for t in range(1, 4):
                        p_send[t, piece, top, 0, inner, :] = numer[t].astype(BF16)
                        p_send[t, piece, top, 1, inner, :] = denom[t].astype(BF16)
                    return 0

                lax.fori_loop(0, HALF // 32, part, 0)
            after, before = ring[half][1], ring[half][3]
            onward = o_sem.at[half, step]
            send(p_send.at[2, piece, 0], o_recv.at[0, piece], send_sem.at[2], onward, after)
            send(p_send.at[2, piece, 1], o_recv.at[1, piece], send_sem.at[2], onward, before)
        return 0

    def combine(step, _):
        for half in (1, 0):
            piece = half * STEPS + step
            wait_for(o_recv.at[:, piece], o_sem.at[half, step])
            for side, t, top in ((0, 1, 0), (1, 3, 1)):
                for kind in range(2):
                    total = p_send[t, piece, top, kind].astype(F32) + o_recv[
                        side, piece, kind
                    ].astype(F32)
                    p_send[t, piece, top, kind] = total.astype(BF16)
                send(
                    p_send.at[t, piece],
                    p_recv.at[side, piece],
                    send_sem.at[2],
                    p_sem.at[half, step],
                    ring[half][t],
                )
        return 0

    def make_template(step, _):
        for half in (1, 0):
            rows = chunk_of(half, step)
            piece = half * STEPS + step
            wait_for(p_recv.at[:, piece], p_sem.at[half, step])
            for top in range(2):

                def part(r, _):
                    at = strip_of(half, step, top * (HALF // 32) + r)
                    inner = pl.ds(pl.multiple_of(r * 32, 32), 32)
                    numer = numer_own[at, :]
                    denom = denom_own[at, :]
                    for side in range(2):
                        numer = numer + p_recv[side, piece, top, 0, inner, :].astype(F32)
                        denom = denom + p_recv[side, piece, top, 1, inner, :].astype(F32)
                    t_all[0, at, :] = (numer / jnp.maximum(denom, 1.0)).astype(BF16)
                    return 0

                lax.fori_loop(0, HALF // 32, part, 0)
            arrive = t_sem.at[half, step]
            send(t_all.at[0, rows], t_all.at[1, rows], send_sem.at[3], arrive, ring[half][1])
            send(t_all.at[0, rows], t_all.at[2, rows], send_sem.at[3], arrive, ring[half][3])
        return 0

    def forward(step, _):
        for half in (1, 0):
            wait_for(t_all.at[pl.ds(1, 2), chunk_of(half, step)], t_sem.at[half, step])
            arrive = f_sem.at[half, step]
            top, low = half_chunk_of(half, step, 0), half_chunk_of(half, step, 1)
            send(t_all.at[1, top], t_all.at[3, top], send_sem.at[3], arrive, ring[half][1])
            send(t_all.at[2, low], t_all.at[3, low], send_sem.at[3], arrive, ring[half][3])
        return 0

    def send_edges():
        for half in range(2):
            column = mirror if half else own
            wide = jnp.concatenate(
                [t_all[0, half * 512 + 64 * b : half * 512 + 64 * b + 64, :] for b in range(8)], 1
            )
            packed = jnp.dot(wide, pack_mat[...], preferred_element_type=F32).astype(BF16)
            for side in range(2):
                e_send[half, side] = packed[:, side * TILE : (side + 1) * TILE]
                peer = lax.rem(column + (31 if side else 1), 32)
                send(e_send.at[half, side], e_recv.at[half, side], send_sem.at[6], e_sem, peer)

    def send_home(src, into, target, step):
        @pl.when(target != own)
        def _():
            send(src, into, send_sem.at[5], x_sem.at[step], target)

        @pl.when(target == own)
        def _():
            pltpu.make_async_copy(src, into, x_sem.at[step]).start()

    def pick_templates(step, _):
        for half in (1, 0):
            klass, slot = places[half]
            rows = chunk_of(half, step)
            wait_for(t_all.at[3, rows], f_sem.at[half, step])
            if half:
                strip = strip_of(1, step, slot * (CHUNK // TILE))
                into = natural.at[strip_of(0, step, slot * (CHUNK // TILE))]
                for held, t in ((0, 0), (1, 1), (3, 2), (2, 3)):
                    send_home(
                        t_all.at[held, strip], into, 8 * lax.rem(slot + 4 - t, 4) + klass, step
                    )
            rel = [
                jnp.full(
                    (32, TILE),
                    jnp.bitwise_and(slot - column_slot(group[half][d], klass) + 4, 3),
                    jnp.int32,
                )
                for d in range(8)
            ]

            def part(r, _):
                at = strip_of(half, step, r)
                values = [t_all[place, at, :] for place in (0, 1, 3, 2)]
                for d in range(8):
                    value = values[0]
                    for t in range(1, 4):
                        value = jnp.where(rel[d] == t, values[t], value)
                    q_send[d, at, :] = value
                return 0

            lax.fori_loop(0, CHUNK // 32, part, 0)
            to_group(half, step, q_send, q_recv, send_sem.at[4], q_sem)
        return 0

    def subtract(step, _):
        for half in (1, 0):
            wait_for(q_recv.at[pl.ds(1, 7), chunk_of(half, step)], q_sem.at[half, step])

            def part(r, _):
                at = strip_of(half, step, r)
                tiles = []
                for i in range(8):
                    d = (8 - i) % 8
                    m = m_send[i, at, :].astype(F32)
                    q = (q_recv if d else q_send)[d, at, :].astype(F32)
                    tiles.append((m - q).astype(BF16))
                for c, tile in enumerate(turned(tiles, 64 - turn[half])):
                    difference_out[at, c * TILE : (c + 1) * TILE] = tile
                return 0

            lax.fori_loop(0, CHUNK // 32, part, 0)
        return 0

    smooth[0:16] = jnp.zeros((16, TILE), BF16)
    smooth[IMG + 16 : IMG + 32] = jnp.zeros((16, TILE), BF16)
    lane_group = lax.div(lax.broadcasted_iota(jnp.int32, (64, TILE), 1), 16)

    def smooth_rows(i):
        half = i // 4
        pieces = []
        for b in range(2 * (i % 4), 2 * (i % 4) + 2):
            here = (natural if half else t_all.at[0])[64 * b : 64 * b + 64, :]
            zero = jnp.zeros((64, TILE), BF16)
            left = jnp.where(lane_group == b, e_recv[half, 0], zero)
            right = jnp.where(lane_group == b, e_recv[half, 1], zero)
            pieces.append(jnp.concatenate([here, left, right], 1))
        got = jnp.dot(jnp.concatenate(pieces, 0), smooth_mat[...], preferred_element_type=F32)
        smooth[16 + TILE * i : 16 + TILE * i + TILE] = got.astype(BF16)

    def filter_rows(i):
        got = jnp.dot(
            filter_mat[...], smooth[TILE * i : TILE * i + 160], preferred_element_type=F32
        )
        power[TILE * i : TILE * i + TILE] = got * got
        power_out[TILE * i : TILE * i + TILE] = (got * got).astype(BF16)

    def send_power(target):
        @pl.when(target != band)
        def _():
            place_in = lax.rem(band - target + 4, 4) - 1
            send(
                power_out.at[pl.ds(256 * target, 256)],
                b_recv.at[place_in],
                send_sem.at[7],
                b_sem,
                own,
                target,
            )

    def upper_detection():
        wait_for(e_recv, e_sem)
        for i in range(4):
            smooth_rows(i)
        wait_for(natural.at[pl.ds(0, CHUNK)], x_sem.at[0])
        smooth_rows(4)
        for i in range(4):
            filter_rows(i)
        send_power(0)
        send_power(1)

    stages = (
        (stage_matched, -AHEAD),
        (reduce_group, 0),
        (combine, 1),
        (make_template, 2),
        (forward, 3),
        (pick_templates, 4),
    )

    def tick(n, _):
        @pl.when(n == STEPS + 3)
        def _():
            upper_detection()

        for stage, lag in stages:
            if lag >= 0:

                @pl.when(jnp.logical_and(n >= lag, n < STEPS + lag))
                def _():
                    stage(n - lag, 0)

            else:

                @pl.when(n < STEPS + lag)
                def _():
                    stage(n - lag, 0)

            if stage is make_template:

                @pl.when(n == STEPS + 1)
                def _():
                    send_edges()

        return 0

    lax.fori_loop(0, AHEAD, stage_matched, 0)
    lax.fori_loop(0, STEPS + 4, tick, 0)
    lax.fori_loop(0, 1, subtract, 0)
    for step in range(1, STEPS):
        wait_for(natural.at[pl.ds(step * CHUNK, CHUNK)], x_sem.at[step])
    for i in range(5, 8):
        smooth_rows(i)
    for i in range(4, 8):
        filter_rows(i)
    send_power(2)
    send_power(3)

    lax.fori_loop(1, STEPS, subtract, 0)
    wait_for(b_recv, b_sem)
    detection_out[...] = (
        power[quarter_of(band), :]
        + b_recv[0].astype(F32)
        + b_recv[1].astype(F32)
        + b_recv[2].astype(F32)
    )
    wait_for(w_send.at[pl.ds(1, 7)], send_sem.at[0])
    wait_for(m_send.at[pl.ds(1, 7)], send_sem.at[1])
    wait_for(p_send.at[pl.ds(1, 3)], send_sem.at[2])
    wait_for(t_all.at[pl.ds(1, 3)], send_sem.at[3])
    wait_for(q_send.at[pl.ds(1, 7)], send_sem.at[4])

    @pl.when(mirror != own)
    def _():
        wait_for(natural, send_sem.at[5])

    @pl.when(mirror == own)
    def _():
        wait_for(natural.at[pl.ds(0, 3 * TILE)], send_sem.at[5])

    wait_for(e_send, send_sem.at[6])
    wait_for(b_recv, send_sem.at[7])


def coadd(picture, variance, planes, sky_columns, basis_rows, basis_cols, coeffs, detect_taps):
    vmem = pl.BlockSpec(memory_space=pltpu.VMEM)
    smem = pl.BlockSpec(memory_space=pltpu.SMEM)
    anyw = pl.BlockSpec(memory_space=pl.ANY)
    tiles = pltpu.VMEM((8, IMG, TILE), BF16)
    arrivals = pltpu.SemaphoreType.DMA((2, STEPS))
    return pl.pallas_call(
        coadd_kernel,
        out_shape=(pltpu.VMEM((IMG, IMG), BF16), pltpu.VMEM((IMG // 4, TILE), F32)),
        in_specs=[anyw, anyw, smem, anyw, vmem, vmem, smem, vmem],
        out_specs=(vmem, vmem),
        scratch_shapes=[
            pltpu.VMEM((IMG, IMG), BF16),
            pltpu.VMEM((IMG, IMG), BF16),
            pltpu.SMEM((4, 8, 32), jnp.int32),
            pltpu.VMEM((8, IMG), F32),
            pltpu.VMEM((2 * TILE, NB * TILE), BF16),
            pltpu.VMEM((TILE, KROWS), BF16),
            pltpu.VMEM((66, NB, 16, IMG), BF16),
            pltpu.VMEM((TILE, IMG), BF16),
            tiles,
            tiles,
            tiles,
            tiles,
            pltpu.VMEM((4, 2 * STEPS, 2, 2, HALF, TILE), BF16),
            pltpu.VMEM((2, 2 * STEPS, 2, 2, HALF, TILE), BF16),
            pltpu.VMEM((2, 2 * STEPS, 2, HALF, TILE), BF16),
            pltpu.VMEM((IMG, TILE), F32),
            pltpu.VMEM((IMG, TILE), F32),
            pltpu.VMEM((4, IMG, TILE), BF16),
            tiles,
            tiles,
            pltpu.VMEM((IMG, TILE), F32),
            pltpu.VMEM((IMG, 2 * TILE), BF16),
            pltpu.VMEM((3 * TILE, TILE), BF16),
            pltpu.VMEM((TILE, 160), BF16),
            pltpu.VMEM((512, TILE), BF16),
            pltpu.VMEM((2, 2, 64, TILE), BF16),
            pltpu.VMEM((2, 2, 64, TILE), BF16),
            pltpu.VMEM((IMG + 32, TILE), BF16),
            pltpu.VMEM((IMG, TILE), F32),
            pltpu.VMEM((IMG, TILE), BF16),
            pltpu.VMEM((3, IMG // 4, TILE), BF16),
            pltpu.SemaphoreType.DMA((3,)),
            pltpu.SemaphoreType.DMA((8,)),
            pltpu.SemaphoreType.DMA((2,)),
            arrivals,
            arrivals,
            arrivals,
            arrivals,
            arrivals,
            arrivals,
            pltpu.SemaphoreType.DMA((STEPS,)),
            pltpu.SemaphoreType.DMA,
            pltpu.SemaphoreType.DMA,
        ],
        compiler_params=pltpu.CompilerParams(
            collective_id=0, has_side_effects=True, vmem_limit_bytes=54 << 20
        ),
        name="coadd",
    )(picture, variance, planes, sky_columns, basis_rows, basis_cols, coeffs, detect_taps)


def body(
    exposures,
    inv_variance,
    mask_planes,
    sky_columns,
    basis_rows,
    basis_cols,
    match_coeffs,
    detect_taps,
):
    difference, detection = coadd(
        exposures[0, 0],
        inv_variance[0, 0],
        mask_planes[0, 0],
        jnp.transpose(sky_columns, (1, 2, 0)),
        basis_rows,
        basis_cols,
        match_coeffs[0],
        detect_taps,
    )
    return (difference[None, None], detection)


def solution(mesh):
    in_specs = (
        P("sky", "band", None, None),
        P("sky", "band", None, None),
        P("sky", "band", None, None),
        P(),
        P(),
        P(),
        P("sky", "band", None),
        P("band", None),
    )
    out_specs = (P("sky", "band", None, None), P("band", "sky"))
    return jax.shard_map(body, mesh=mesh, in_specs=in_specs, out_specs=out_specs, check_vma=False)
```
